32 devices in a mesh: samples: 8 (over y, x, core), cols: 4 (over z).
Axes of the slice: x: 2, y: 2, z: 4, core: 2. Of those that a mesh axis runs over, the one named last changes fastest.
Arguments:
- features: bfloat16 [32768, 440], P('samples'), may hold values from -6 to 6
- labels: int32 [32768], P('samples'), may hold values from 0 to 146
- weights: float32 [32768, 147], P('samples'), may hold values from -6 to 6
- block_order: int32 [8], replicated, may hold values from 0 to 7, each once
- block_starts: int32 [8], replicated, may hold values from 0 to 3584
- inverses: float32 [4, 4096, 4096], P(None, 'samples', 'cols'), may hold values from -0.125 to 1.5
Outputs:
- new_weights: float32 [32768, 147], P('samples')
The draws below stay inside these ranges and needn't reach their ends.
All inputs are finite; a program needn't handle non-finite values.
Results may differ from the reference program's by a relative error of at most 0.0005.
Values may be sent and summed in bfloat16 or wider, within the bound.
No kernel may reach another device: no remote copies, remote signals or barrier semaphores. Data moves between devices by JAX's collectives and lax.ppermute only.
A program may use at most 128 MiB of HBM per device.

```python
import math
import jax
import jax.numpy as jnp
from jax import lax

F = 440
C = 147
B = 4096
NUPD = 4
ROWS_DEV = 4096
N = 32768
NBLK = 8
RB = 512
QI = 128
CB = 1024
N_SAMPLES = 8


def draw_features(key, part):
    clusters = 32
    first, second, third = jax.random.split(jax.random.fold_in(key, 11), 3)
    member = jax.random.randint(second, (N,), 0, clusters)
    centers = jax.random.normal(first, (clusters, F), jnp.float32) * 1.5 ** 0.5
    spread = jax.random.normal(third, (N, F), jnp.float32) * 0.5 ** 0.5
    values = jnp.take(centers, member, axis=0) + spread
    return jnp.clip(values, -6.0, 6.0).astype(jnp.bfloat16)


def draw_inverses(key, part):

    def single(subkey):
        first, second = jax.random.split(subkey)
        diagonal = jax.random.uniform(first, (B,), jnp.float32, 0.5, 1.5)
        spread = jax.random.truncated_normal(second, -4.0, 4.0, (B, B), jnp.float32) * (0.5 / B ** 0.5)
        unit = jnp.eye(B, dtype=jnp.float32)
        square = spread * (1.0 - unit) + unit * diagonal[None, :]
        index = jnp.arange(B, dtype=jnp.int32)
        groups = RB // QI
        group = index // (B // groups)
        owner = index % (B // groups) // QI
        inner = index % QI
        source = (owner * RB + group * QI + inner).astype(jnp.int32)
        return square[:, source]
    return jax.lax.map(single, jax.random.split(jax.random.fold_in(key, 7), NUPD))


def plant(drawn, key, least, top_value):
    spot = [jax.random.randint(jax.random.fold_in(key, axis), (), 0, length) for axis, length in enumerate(drawn.shape)]
    widest = drawn.shape.index(max(drawn.shape))
    neighbour = spot[:widest] + [(spot[widest] + 1) % drawn.shape[widest]] + spot[widest + 1:]
    return drawn.at[tuple(spot)].set(least).at[tuple(neighbour)].set(top_value)


def block_scale(rng, dims, pieces, low, high):
    def one(axis_at, parts):
        draws = jax.random.uniform(jax.random.fold_in(jax.random.fold_in(rng, 6), axis_at), (parts,), jnp.float32, low / len(pieces), high / len(pieces))
        return jnp.repeat(jnp.exp(draws), dims[axis_at] // parts).reshape((-1,) + (1,) * (len(dims) - axis_at - 1))

    level = one(*pieces[0])
    for cut in pieces[1:]:
        level = level * one(*cut)
    return level


def noise(key, extent, scale, bound, cuts=(), kind=jnp.bfloat16):
    factor_of = block_scale(key, extent, cuts, -0.22, 0.18) if cuts else 1.0
    drawn = jax.random.normal(key, extent, jnp.float32) * scale * factor_of
    return jnp.minimum(jnp.maximum(drawn, -bound), bound).astype(kind)


def setup_inputs(seed: int = 0) -> dict:
    key_of = jax.random.split(jax.random.key(seed), 7)
    return {
        "features": draw_features(jax.random.fold_in(key_of[6], 71), 0),
        "labels": plant(jax.random.randint(key_of[1], (N,), 0, C), jax.random.fold_in(key_of[1], 1), 0, C - 1).astype(jnp.int32),
        "weights": noise(key_of[2], (N, C), 1.0, 6.0, ((0, 8),), jnp.float32),
        "block_order": jax.random.permutation(key_of[3], NBLK).astype(jnp.int32),
        "block_starts": plant(jax.random.randint(key_of[4], (NBLK,), 0, ROWS_DEV - RB + 1), jax.random.fold_in(key_of[4], 1), 0, ROWS_DEV - RB).astype(jnp.int32),
        "inverses": draw_inverses(jax.random.fold_in(key_of[6], 71), 0),
    }


RIDGE = 0.5

def member_rows(start):
    shard = jnp.arange(N_SAMPLES, dtype=jnp.int32)
    slot = jnp.arange(RB, dtype=jnp.int32)
    rows_r = (shard[:, None] * ROWS_DEV + start + slot[None, :]).reshape(-1).astype(jnp.int32)
    index = jnp.arange(B, dtype=jnp.int32)
    group = index // CB
    owner = index % CB // QI
    inner = index % QI
    rows_q = (owner * ROWS_DEV + start + group * QI + inner).astype(jnp.int32)
    return (rows_r, rows_q)

def block_products(features, current, rows_q):
    chosen = features[rows_q].astype(jnp.float32)
    chosen_norms = lax.optimization_barrier(jnp.sum(chosen * chosen, axis=1))
    shaped_x = features.reshape(N_SAMPLES, ROWS_DEV, F)
    shaped_w = current.reshape(N_SAMPLES, ROWS_DEV, C)

    def accumulate(total, pair):
        block_x, block_w = pair
        values = block_x.astype(jnp.float32)
        inner = jnp.dot(values, chosen.T, precision=lax.Precision.HIGHEST)
        norms = lax.optimization_barrier(jnp.sum(values * values, axis=1))
        panel = jnp.exp((2.0 * inner - norms[:, None] - chosen_norms[None, :]) / F)
        return (total + jnp.dot(panel.T, block_w, precision=lax.Precision.HIGHEST), None)
    total, unused = lax.scan(accumulate, jnp.zeros((B, C), jnp.float32), (shaped_x, shaped_w))
    return total

def reference(features, labels, weights, block_order, block_starts, inverses):
    current = weights
    scale = 1.0 / math.sqrt(N)
    classes = jnp.arange(C, dtype=jnp.int32)
    for step in range(NUPD):
        start = block_starts[block_order[step]]
        rows_r, rows_q = member_rows(start)
        products = block_products(features, current, rows_q)
        onehot = (labels[rows_q][:, None] == classes[None, :]).astype(jnp.float32)
        residual = onehot - scale * products - RIDGE * current[rows_q]
        delta = jnp.dot(inverses[step], residual, precision=lax.Precision.HIGHEST)
        current = current.at[rows_r].add(delta)
    return current
```

```python
import math

import jax
import jax.numpy as jnp
from jax import lax
from jax.experimental import pallas as pl
from jax.experimental.pallas import tpu as pltpu
from jax.sharding import PartitionSpec as P

RIDGE = 0.5
F32, BF16 = jnp.float32, jnp.bfloat16
VMEM = pl.BlockSpec(memory_space=pltpu.VMEM)
SMEM = pl.BlockSpec(memory_space=pltpu.SMEM)
NT = (((1,), (1,)), ((), ()))


def up(value, unit):
    return -(-value // unit) * unit


def swap(value, axis, mask):
    size = lax.axis_size(axis)
    return lax.ppermute(value, axis, [(i, i ^ mask) for i in range(size)])


def rounded(value):
    return lax.reduce_precision(value, 8, 7)


def split3(value):
    high = rounded(value)
    middle = rounded(value - high)
    low = value - high - middle
    return [part.astype(BF16) for part in (high, middle, low)]


def extend(rows, query):
    wide = rows.astype(F32)
    halves = split3(-0.5 * jnp.sum(wide * wide, axis=1, keepdims=True))
    ones = [jnp.ones_like(halves[0])] * 3
    tail = ones + halves if query else halves + ones
    joined = jnp.concatenate([rows] + tail, axis=1)
    return jnp.pad(joined, ((0, 0), (0, up(joined.shape[1], 128) - joined.shape[1])))


def params(kib, **more):
    return pltpu.CompilerParams(vmem_limit_bytes=kib * 1024, **more)


def assemble(pieces, places):
    count = len(pieces)
    rows, depth = pieces[0].shape

    def kernel(place_ref, *refs):
        for index in range(count):
            start = pl.multiple_of(place_ref[index] * rows, rows)
            refs[count][pl.ds(start, rows), :] = refs[index][...]

    return pl.pallas_call(
        kernel,
        out_shape=jax.ShapeDtypeStruct((count * rows, depth), BF16),
        in_specs=[SMEM] + [VMEM] * count,
        out_specs=VMEM,
        compiler_params=params(8 * 1024),
        name="assemble",
    )(places, *pieces)


def heavy(keys, weights2, stretch, base, factor, scale, block, first, last):
    depth = keys.shape[1]
    columns = stretch.shape[0]
    half = columns // 2
    doubled = weights2.shape[0]
    classes = doubled // 2
    wide = min(256, half)

    def kernel(keys_ref, weights_ref, stretch_ref, keep_in, send_in, keep_ref, send_ref, total):
        step = pl.program_id(0)

        @pl.when(step == 0)
        def _():
            total[...] = jnp.zeros_like(total)

        for j in range(columns // wide):
            span = slice(j * wide, (j + 1) * wide)
            inner = lax.dot_general(
                keys_ref[...], stretch_ref[span, :], NT, preferred_element_type=F32
            )
            panel = jnp.exp2(inner * factor).astype(BF16)
            total[:, span] += jnp.dot(weights_ref[...], panel, preferred_element_type=F32)

        @pl.when(step == pl.num_programs(0) - 1)
        def _():
            keep_ref[...] = keep_in[...] - scale * (total[:classes, :half] + total[classes:, :half])
            send_ref[...] = send_in[...] - scale * (total[:classes, half:] + total[classes:, half:])

    shape = jax.ShapeDtypeStruct((classes, half), F32)
    whole = pl.BlockSpec((classes, half), lambda i: (0, 0))
    count = last - first
    return pl.pallas_call(
        kernel,
        grid=(count,),
        in_specs=[
            pl.BlockSpec((block, depth), lambda i: (i + first, 0)),
            pl.BlockSpec((doubled, block), lambda i: (0, i + first)),
            pl.BlockSpec((columns, depth), lambda i: (0, 0)),
            whole,
            whole,
        ],
        out_specs=[whole, whole],
        out_shape=[shape, shape],
        scratch_shapes=[pltpu.VMEM((doubled, columns), F32)],
        compiler_params=params(16 * 1024, dimension_semantics=("arbitrary",)),
        cost_estimate=pl.CostEstimate(
            flops=2 * count * block * columns * (depth + doubled),
            transcendentals=count * block * columns,
            bytes_accessed=2 * count * block * (depth + doubled) + 2 * columns * depth,
        ),
        name="heavy",
    )(keys, weights2, stretch, *base)


def tiles(members, stretch, factor):
    count, rows, depth = members.shape
    columns = stretch.shape[0]

    def kernel(members_ref, stretch_ref, out_ref):
        inner = lax.dot_general(members_ref[...], stretch_ref[...], NT, preferred_element_type=F32)
        out_ref[...] = jnp.exp2(inner * factor).astype(BF16)

    return pl.pallas_call(
        kernel,
        grid=(count,),
        in_specs=[
            pl.BlockSpec((None, rows, depth), lambda i: (i, 0, 0)),
            pl.BlockSpec((columns, depth), lambda i: (0, 0)),
        ],
        out_specs=pl.BlockSpec((None, rows, columns), lambda i: (i, 0, 0)),
        out_shape=jax.ShapeDtypeStruct((count, rows, columns), BF16),
        compiler_params=params(10 * 1024, dimension_semantics=("arbitrary",)),
        cost_estimate=pl.CostEstimate(
            flops=2 * count * rows * columns * depth,
            transcendentals=count * rows * columns,
            bytes_accessed=2 * count * rows * (columns + depth) + 2 * columns * depth,
        ),
        name="tiles",
    )(members, stretch)


def correct(base, parts, tile, index, where, scale, window):
    classes, half = base[0].shape
    rows, columns = tile.shape[1:]
    lanes = rows // len(parts)

    def kernel(where_ref, tile_ref, keep_in, send_in, *refs):
        sides = refs[: sum(len(pair) for pair in parts)]
        keep_ref, send_ref, delta_ref, sums = refs[len(sides) :]
        at = 0
        for k, pair in enumerate(parts):
            value = sides[at][...]
            for more in range(1, len(pair)):
                value = value + sides[at + more][...]
            at += len(pair)
            delta_ref[:, k * lanes : (k + 1) * lanes] = value
        delta = delta_ref[...]
        high = delta.astype(BF16)
        rest = delta - high.astype(F32)
        middle = rest.astype(BF16)
        low = (rest - middle.astype(F32)).astype(BF16)
        both = jnp.concatenate([high, middle], axis=0)
        product = jnp.dot(both, tile_ref[0], preferred_element_type=F32)
        sums[...] = -scale * (product[:classes] + product[classes:])
        offset, slot, inside = where_ref[0], where_ref[1], where_ref[2]
        row = lax.broadcasted_iota(jnp.int32, (rows, window), 0)
        lane = lax.broadcasted_iota(jnp.int32, (rows, window), 1) - inside
        match = (row == lane + offset) & (lane >= 0) & (lane < where_ref[3])
        chosen = jnp.where(match, 1.0, 0.0).astype(BF16)
        picked = jnp.dot(
            jnp.concatenate([high, middle, low], axis=0), chosen, preferred_element_type=F32
        )
        picked = picked[:classes] + picked[classes : 2 * classes] + picked[2 * classes :]
        at = pl.ds(pl.multiple_of(slot * window, window), window)
        sums[:, at] = sums[:, at] - RIDGE * picked
        keep_ref[...] = keep_in[...] + sums[:, :half]
        send_ref[...] = send_in[...] + sums[:, half:]

    shape = jax.ShapeDtypeStruct((classes, half), F32)
    flat = [side for pair in parts for side in pair]
    grid_spec = pltpu.PrefetchScalarGridSpec(
        num_scalar_prefetch=1,
        grid=(1,),
        in_specs=[pl.BlockSpec((1, rows, columns), lambda i, w: (index, 0, 0))]
        + [pl.BlockSpec(value.shape, lambda i, w: (0, 0)) for value in list(base) + flat],
        out_specs=[pl.BlockSpec((classes, half), lambda i, w: (0, 0))] * 2
        + [pl.BlockSpec((classes, rows), lambda i, w: (0, 0))],
        scratch_shapes=[pltpu.VMEM((classes, columns), F32)],
    )
    return pl.pallas_call(
        kernel,
        grid_spec=grid_spec,
        out_shape=[shape, shape, jax.ShapeDtypeStruct((classes, rows), F32)],
        compiler_params=params(16 * 1024, dimension_semantics=("arbitrary",)),
        cost_estimate=pl.CostEstimate(
            flops=4 * classes * rows * columns, transcendentals=0, bytes_accessed=2 * rows * columns
        ),
        name="correct",
    )(where, tile, *base, *flat)


def apply_half(high, low, index, residual, start, lanes):
    classes, depth = residual.shape
    rows = high.shape[1]
    count = rows // lanes

    def kernel(high_ref, low_ref, residual_ref, *refs):
        value = residual_ref[...]
        top = value.astype(BF16)
        rest = (value - top.astype(F32)).astype(BF16)
        both = jnp.concatenate([top, rest], axis=0)
        product = lax.dot_general(both, high_ref[0], NT, preferred_element_type=F32)
        total = product[:classes] + product[classes:]
        total = total + lax.dot_general(top, low_ref[0], NT, preferred_element_type=F32)
        for k in range(count):
            piece = total[:, k * lanes : (k + 1) * lanes]
            if start is not None:
                piece = piece + refs[k][...]
            refs[len(refs) - count + k][...] = piece

    matrix = pl.BlockSpec((1, rows, depth), lambda i: (index, 0, 0))
    side = pl.BlockSpec((classes, lanes), lambda i: (0, 0))
    return pl.pallas_call(
        kernel,
        grid=(1,),
        in_specs=[matrix, matrix, pl.BlockSpec((classes, depth), lambda i: (0, 0))]
        + ([side] * count if start is not None else []),
        out_specs=[side] * count,
        out_shape=[jax.ShapeDtypeStruct((classes, lanes), F32)] * count,
        compiler_params=params(12 * 1024, dimension_semantics=("arbitrary",)),
        cost_estimate=pl.CostEstimate(
            flops=6 * classes * rows * depth, transcendentals=0, bytes_accessed=4 * rows * depth
        ),
        name="apply_half",
    )(high, low, residual, *(start or []))


def exchange(parts, axis, orders):
    rounds = len(orders[0])
    for step in range(rounds):
        got = [swap(part, axis, order[step]) for part, order in zip(parts, orders)]
        if step == rounds - 1:
            return [[part, other] for part, other in zip(parts, got)]
        parts = [part + other for part, other in zip(parts, got)]


def rotations(masks, count):
    return [masks[k % len(masks) :] + masks[: k % len(masks)] for k in range(count)]


def body(features, labels, weights, block_order, block_starts, inverses):
    rows, width = features.shape
    updates, span, stretch_rows = inverses.shape
    kinds = weights.shape[1]
    shards, groups = lax.axis_size("samples"), lax.axis_size("cols")
    shard, group = lax.axis_index("samples"), lax.axis_index("cols")
    core = shard % 2
    piece = stretch_rows // shards
    half = stretch_rows // 2
    window = max(piece, 128)
    classes = up(kinds, 8)
    scale = 1.0 / math.sqrt(rows * shards)
    factor = 2.0 / (width * math.log(2.0))
    block = 512
    starts = [block_starts[block_order[step]] for step in range(updates)]
    own_starts = [start + group * piece for start in starts]
    flip = core * (shards // 2)
    place = shard ^ flip
    inside = place * piece % window
    slot = place * piece // window

    far = [mask for mask in range(2, shards, 2)]
    places = jnp.stack([shard ^ mask ^ flip for mask in [0] + far] + [shard ^ 1 ^ mask ^ flip for mask in [0] + far])

    def gather(step):
        local = extend(lax.dynamic_slice_in_dim(features, own_starts[step], piece, 0), True)
        mine = [local] + [swap(local, "samples", mask) for mask in far]
        mine = jnp.concatenate([value[None] for value in mine], axis=0)
        other = swap(mine, "samples", 1)
        pieces = [mine[k] for k in range(len(far) + 1)] + [other[k] for k in range(len(far) + 1)]
        return assemble(pieces, places)

    keys = extend(features, False)
    turned = jnp.pad(weights.T, ((0, classes - kinds), (0, 0)))
    top = rounded(turned)
    weights2 = jnp.concatenate([top.astype(BF16), (turned - top).astype(BF16)], axis=0)

    def own(step):
        before = lax.dynamic_slice_in_dim(weights, own_starts[step], piece, 0)
        kind = lax.dynamic_slice_in_dim(labels, own_starts[step], piece, 0)
        hot = (kind[None, :] == jnp.arange(classes, dtype=jnp.int32)[:, None]).astype(F32)
        value = hot - RIDGE * jnp.pad(before.T, ((0, classes - kinds), (0, 0)))
        placed = jnp.zeros((classes, stretch_rows), F32)
        placed = lax.dynamic_update_slice(placed, value, (0, place * piece))
        return placed[:, :half], placed[:, half:]

    def inverse_half(side):
        part = lax.dynamic_slice_in_dim(inverses, side * half, half, 2)
        high = rounded(part)
        return high.astype(BF16), (part - high).astype(BF16)

    mine_inverse, other_inverse = inverse_half(core), inverse_half(1 - core)
    members = jnp.stack(
        [lax.dynamic_slice_in_dim(keys, start, span, 0) for start in starts[:-1]]
    )
    sample_masks = [1 << bit for bit in range(1, shards.bit_length() - 1)]
    col_masks = [(2 << bit) - 1 for bit in range(groups.bit_length() - 1)]
    sample_orders, col_orders = rotations(sample_masks, 2), rotations(col_masks, 2)
    quarter, lanes = half // 2, span // 2

    stretches = [gather(step) for step in range(updates)]
    bases = [
        heavy(keys, weights2, stretches[step], own(step), factor, scale, block, 0, rows // block)
        for step in range(updates)
    ]
    tile_sets = [None] + [
        tiles(members[:step], stretches[step], factor) for step in range(1, updates)
    ]
    current = weights
    for step in range(updates):
        keep, send = bases[step]
        keep = keep + swap(send, "samples", 1)
        pairs = exchange([keep[:, :quarter], keep[:, quarter:]], "samples", sample_orders)
        residual = jnp.concatenate([a + b for a, b in pairs], axis=1)
        other = swap(residual, "samples", 1)
        partial = apply_half(*mine_inverse, step, residual, None, lanes)
        partial = apply_half(*other_inverse, step, other, partial, lanes)
        pairs = exchange(partial, "cols", col_orders)
        if step < updates - 1:
            for later in range(step + 1, updates):
                where = jnp.stack([own_starts[later] - starts[step], slot, inside, jnp.int32(piece)])
                keep, send, delta = correct(
                    bases[later], pairs, tile_sets[later], step, where, scale, window
                )
                bases[later] = (keep, send)
                if later == step + 1:
                    first_delta = delta
                    pairs = [[delta]]
            delta = first_delta
        else:
            delta = jnp.concatenate([a + b for a, b in pairs], axis=1)
        before = lax.dynamic_slice_in_dim(current, starts[step], span, 0)
        current = lax.dynamic_update_slice_in_dim(
            current, before + delta[:kinds].T, starts[step], 0
        )
    return current


def solution(mesh):
    return jax.shard_map(
        body,
        mesh=mesh,
        in_specs=(
            P("samples", None),
            P("samples"),
            P("samples", None),
            P(),
            P(),
            P(None, "samples", "cols"),
        ),
        out_specs=P("samples", None),
        check_vma=False,
    )
```

```python
import math

import jax
import jax.numpy as jnp
from jax import lax
from jax.experimental import pallas as pl
from jax.experimental.pallas import tpu as pltpu
from jax.sharding import PartitionSpec as P

RIDGE = 0.5
F32, BF16, I32 = jnp.float32, jnp.bfloat16, jnp.int32
LANES = 128
VMEM = pl.BlockSpec(memory_space=pltpu.VMEM)
SMEM = pl.BlockSpec(memory_space=pltpu.SMEM)
NT = (((1,), (1,)), ((), ()))


def up(value, unit):
    return -(-value // unit) * unit


def of(shape, kind=F32):
    return jax.ShapeDtypeStruct(shape, kind)


def swap(value, axis, mask):
    size = lax.axis_size(axis)
    return lax.ppermute(value, axis, [(i, i ^ mask) for i in range(size)])


def params(mib, **more):
    return pltpu.CompilerParams(vmem_limit_bytes=mib << 20, **more)


def call(kernel, out, operands, specs=None, mib=8, scratch=(), flops=0, exps=0, moved=0, aliases=None, name=None):
    count = len(operands)
    return pl.pallas_call(
        kernel,
        out_shape=out,
        in_specs=specs or [VMEM] * count,
        out_specs=jax.tree.map(lambda _: VMEM, out),
        scratch_shapes=list(scratch),
        input_output_aliases=aliases or {},
        compiler_params=params(mib),
        cost_estimate=pl.CostEstimate(flops=flops, transcendentals=exps, bytes_accessed=moved),
        name=name,
    )(*operands)


def halves_of_norm(wide):
    value = -0.5 * jnp.sum(wide * wide, axis=0, keepdims=True)
    high = value.astype(BF16).astype(F32)
    middle = (value - high).astype(BF16).astype(F32)
    return high, middle, value - high - middle


def extended(wide, query):
    row = lax.broadcasted_iota(I32, (8, wide.shape[1]), 0)
    tail = jnp.zeros(row.shape, F32)
    first = 3 if query else 0
    for k, part in enumerate(halves_of_norm(wide)):
        tail = jnp.where(row == first + k, part, tail)
        tail = jnp.where(row == 3 - first + k, 1.0, tail)
    return jnp.concatenate([wide, tail], axis=0)


def views(array, count, offset):
    rows, lanes = array.shape
    last = lanes // LANES - 1

    def at(k):
        return pl.BlockSpec((rows, LANES), lambda i, *scalars: (0, jnp.minimum(offset(i, *scalars) // LANES + k, last)))

    return [at(k) for k in range(count)]


def windowed(kernel, scalars, grid, in_specs, out_specs, out, operands, aliases=None, scratch=(), mib=8, name=None):
    return pl.pallas_call(
        kernel,
        grid_spec=pltpu.PrefetchScalarGridSpec(
            num_scalar_prefetch=len(scalars),
            grid=grid,
            in_specs=in_specs,
            out_specs=out_specs,
            scratch_shapes=list(scratch),
        ),
        out_shape=out,
        input_output_aliases=aliases or {},
        compiler_params=params(mib, dimension_semantics=("arbitrary",)),
        cost_estimate=pl.CostEstimate(flops=1 << 20, transcendentals=0, bytes_accessed=1 << 20),
        name=name,
    )(*scalars, *operands)


def member_rows(turned, scalars, start, count, query):
    depth = turned.shape[0] + 8
    seen = up(count, LANES) // LANES + 1

    def kernel(*refs):
        shift = start(*refs[: len(scalars)]) % LANES
        blocks, out_ref = refs[len(scalars) : -1], refs[-1]
        wide = jnp.concatenate([block[...].astype(F32) for block in blocks], axis=1)
        wide = extended(wide, query).astype(BF16)
        shape = (seen * LANES, count) if query else (count, seen * LANES)
        lane = lax.broadcasted_iota(I32, shape, 0 if query else 1)
        member = lax.broadcasted_iota(I32, shape, 1 if query else 0)
        chosen = jnp.where(lane == member + shift, 1.0, 0.0).astype(BF16)
        if query:
            rows = jnp.dot(wide, chosen, preferred_element_type=F32)
        else:
            rows = lax.dot_general(chosen, wide, NT, preferred_element_type=F32)
        out_ref[...] = rows.astype(BF16)

    shape = (depth, count) if query else (count, depth)
    return windowed(
        kernel,
        scalars,
        (1,),
        views(turned, seen, lambda i, *refs: start(*refs)),
        pl.BlockSpec(shape, lambda i, *refs: (0, 0)),
        of(shape, BF16),
        [turned] * seen,
        name="member_rows",
    )


def own_terms(weights, labels, scalars, start, classes, piece, window, inside):
    kinds = weights.shape[0]
    last = labels.shape[0] - 1

    def kernel(*refs):
        known = refs[: len(scalars)]
        low_ref, high_ref, labels_ref, out_ref = refs[len(scalars) :]
        first = start(*known)
        block, begin = first // LANES, inside(*known)
        turn = (begin - first % LANES + 2 * LANES) % (2 * LANES)
        both = pltpu.roll(jnp.concatenate([low_ref[...], high_ref[...]], axis=1), turn, 1)[:, :LANES]
        rows = [labels_ref[pl.ds(jnp.minimum(block + k, last), 1), :] for k in range(2)]
        rows = jnp.broadcast_to(jnp.concatenate(rows, axis=1), (8, 2 * LANES))
        label = pltpu.roll(rows, turn, 1)[:1, :LANES]
        hot = jnp.where(lax.broadcasted_iota(I32, (kinds, LANES), 0) == label, 1.0, 0.0)
        lane = lax.broadcasted_iota(I32, (kinds, LANES), 1) - begin
        value = jnp.where((lane >= 0) & (lane < piece), hot - RIDGE * both, 0.0)
        out_ref[...] = jnp.concatenate([value, jnp.zeros((classes - kinds, LANES), F32)], axis=0)

    return windowed(
        kernel,
        scalars,
        (1,),
        views(weights, 2, lambda i, *refs: start(*refs))
        + [pl.BlockSpec(labels.shape, lambda i, *refs: (0, 0))],
        pl.BlockSpec((classes, window), lambda i, *refs: (0, 0)),
        of((classes, window)),
        [weights, weights, labels],
        name="own_terms",
    )


def prepare(turned, weights, classes):
    width, rows = turned.shape
    kinds = weights.shape[0]
    depth, block = width + 8, 512

    def kernel(turned_ref, weights_ref, keys_ref, parts_ref, copy_ref):
        wide = extended(turned_ref[...].astype(F32), False)
        keys_ref[...] = wide.T.astype(BF16)
        value = weights_ref[...]
        copy_ref[...] = value
        value = jnp.concatenate([value, jnp.zeros((classes - kinds, block), F32)], axis=0)
        high = value.astype(BF16).astype(F32)
        parts_ref[...] = jnp.concatenate([high, value - high], axis=0).astype(BF16)

    return pl.pallas_call(
        kernel,
        grid=(rows // block,),
        in_specs=[
            pl.BlockSpec((width, block), lambda i: (0, i)),
            pl.BlockSpec((kinds, block), lambda i: (0, i)),
        ],
        out_specs=[
            pl.BlockSpec((block, depth), lambda i: (i, 0)),
            pl.BlockSpec((2 * classes, block), lambda i: (0, i)),
            pl.BlockSpec((kinds, block), lambda i: (0, i)),
        ],
        out_shape=[of((rows, depth), BF16), of((2 * classes, rows), BF16), of((kinds, rows))],
        compiler_params=params(12, dimension_semantics=("arbitrary",)),
        cost_estimate=pl.CostEstimate(flops=1 << 20, transcendentals=0, bytes_accessed=16 << 20),
        name="prepare",
    )(turned, weights)


def split_inverse(inverses, index, ids):
    rows, columns = inverses.shape[1:]
    half = columns // 2

    def kernel(ids_ref, *refs):
        for k in range(2):
            value = refs[k][0]
            high = value.astype(BF16)
            refs[2 + 2 * k][...] = high
            refs[3 + 2 * k][...] = (value - high.astype(F32)).astype(BF16)

    def side(k):
        return pl.BlockSpec((1, rows, half), lambda i, ids_ref: (index, 0, (ids_ref[0] + k) % 2))

    return windowed(
        kernel,
        [ids],
        (1,),
        [side(0), side(1)],
        [pl.BlockSpec((rows, half), lambda i, ids_ref: (0, 0))] * 4,
        [of((rows, half), BF16)] * 4,
        [inverses, inverses],
        mib=10,
        name="split_inverse",
    )


def assemble(pieces, ids, place):
    count = len(pieces)
    depth, lanes = pieces[0].shape

    def kernel(ids_ref, *refs):
        for index in range(count):
            start = pl.multiple_of(place(ids_ref, index) * lanes, LANES)
            refs[count][:, pl.ds(start, lanes)] = refs[index][...]

    return call(
        kernel, of((depth, count * lanes), BF16), [ids] + pieces, [SMEM] + [VMEM] * count, mib=4, name="assemble"
    )


def heavy(keys, parts, stretch, base, own, ids, slot, factor, scale, first, last):
    depth = keys.shape[1]
    columns = stretch.shape[1]
    half = columns // 2
    quarter = half // 2
    doubled = parts.shape[0]
    classes = doubled // 2
    block = (last - first) // max(1, (last - first) // 1024)
    side = block // 2
    wide = min(256, columns)
    window = own.shape[1] if own is not None else 0

    def kernel(ids_ref, keys_ref, parts_ref, stretch_ref, *refs):
        given = refs[: 1 if base is None else 3]
        a_ref, b_ref, send_ref, total, front, back, out = refs[len(given) :]

        def fill(panel, start):
            lhs = keys_ref[pl.ds(start, side), :]
            for j in range(columns // wide):
                span = slice(j * wide, (j + 1) * wide)
                inner = jnp.dot(lhs, stretch_ref[:, span], preferred_element_type=F32)
                panel[:, span] = jnp.exp2(inner * factor).astype(BF16)

        def drain(panel, start):
            lhs = parts_ref[:, pl.ds(start, side)]
            for j in range(columns // wide):
                span = slice(j * wide, (j + 1) * wide)
                total[:, span] += jnp.dot(lhs, panel[:, span], preferred_element_type=F32)

        total[...] = jnp.zeros_like(total)
        fill(front, first)

        def step(i, carry):
            start = pl.multiple_of(first + i * block, block)
            fill(back, start + side)
            drain(front, start)
            fill(front, start + block)
            drain(back, start + side)
            return carry

        count = (last - first) // block
        lax.fori_loop(0, count - 1, step, 0)
        fill(back, last - side)
        drain(front, last - block)
        drain(back, last - side)
        out[...] = -scale * (total[:classes] + total[classes:])
        if base is None:
            at = pl.ds(pl.multiple_of(slot(ids_ref) * window, LANES), window)
            out[:, at] = out[:, at] + given[0][...]
            a_ref[...] = out[:, :quarter]
            b_ref[...] = out[:, quarter:half]
            send_ref[...] = out[:, half:]
        else:
            a_ref[...] = given[0][...] + out[:, :quarter]
            b_ref[...] = given[1][...] + out[:, quarter:half]
            send_ref[...] = given[2][...] + out[:, half:]

    extra = [own] if base is None else list(base)
    count = last - first
    return call(
        kernel,
        [of((classes, quarter)), of((classes, quarter)), of((classes, half))],
        [ids, keys, parts, stretch] + extra,
        [SMEM] + [VMEM] * (3 + len(extra)),
        mib=16,
        scratch=[
            pltpu.VMEM((doubled, columns), F32),
            pltpu.VMEM((side, columns), BF16),
            pltpu.VMEM((side, columns), BF16),
            pltpu.VMEM((classes, columns), F32),
        ],
        flops=2 * count * columns * (depth + doubled),
        exps=count * columns,
        moved=2 * count * (depth + doubled) + 2 * columns * depth,
        name="heavy",
    )


def tile_of(members, stretch, factor):
    rows, depth = members.shape
    columns = stretch.shape[1]

    def kernel(members_ref, stretch_ref, out_ref):
        inner = jnp.dot(members_ref[...], stretch_ref[...], preferred_element_type=F32)
        out_ref[...] = jnp.exp2(inner * factor).astype(BF16)

    return call(
        kernel,
        of((rows, columns), BF16),
        [members, stretch],
        flops=2 * rows * columns * depth,
        exps=rows * columns,
        moved=2 * rows * (columns + depth) + 2 * columns * depth,
        name="tile",
    )


def correct(base, sides, tile, scalars, offset, slot, inside, piece, window, scale):
    a, b, send = base
    classes, quarter = a.shape
    half = 2 * quarter
    rows, columns = tile.shape
    lanes = rows // len(sides)
    flat = [value for part in sides for value in part]

    def kernel(*refs):
        known = refs[: len(scalars)]
        tile_ref, a_in, b_in, send_in = refs[len(scalars) : len(scalars) + 4]
        given = refs[len(scalars) + 4 : len(scalars) + 4 + len(flat)]
        a_ref, b_ref, send_ref, delta_ref, sums = refs[len(scalars) + 4 + len(flat) :]
        at = 0
        for k, part in enumerate(sides):
            value = given[at][...]
            for more in range(1, len(part)):
                value = value + given[at + more][...]
            at += len(part)
            delta_ref[:, k * lanes : (k + 1) * lanes] = value
        delta = delta_ref[...]
        high = delta.astype(BF16)
        rest = delta - high.astype(F32)
        middle = rest.astype(BF16)
        low = (rest - middle.astype(F32)).astype(BF16)
        both = jnp.concatenate([high, middle], axis=0)
        product = jnp.dot(both, tile_ref[...], preferred_element_type=F32)
        sums[...] = -scale * (product[:classes] + product[classes:])
        row = lax.broadcasted_iota(I32, (rows, window), 0)
        lane = lax.broadcasted_iota(I32, (rows, window), 1) - inside(*known)
        match = (row == lane + offset(*known)) & (lane >= 0) & (lane < piece)
        chosen = jnp.where(match, 1.0, 0.0).astype(BF16)
        picked = jnp.dot(jnp.concatenate([both, low], axis=0), chosen, preferred_element_type=F32)
        picked = picked[:classes] + picked[classes : 2 * classes] + picked[2 * classes :]
        span = pl.ds(pl.multiple_of(slot(*known) * window, LANES), window)
        sums[:, span] = sums[:, span] - RIDGE * picked
        a_ref[...] = a_in[...] + sums[:, :quarter]
        b_ref[...] = b_in[...] + sums[:, quarter:half]
        send_ref[...] = send_in[...] + sums[:, half:]

    return call(
        kernel,
        [of(a.shape), of(b.shape), of(send.shape), of((classes, rows))],
        list(scalars) + [tile, a, b, send] + flat,
        [SMEM] * len(scalars) + [VMEM] * (4 + len(flat)),
        mib=10,
        scratch=[pltpu.VMEM((classes, columns), F32)],
        flops=4 * classes * rows * columns,
        moved=2 * rows * columns,
        name="correct",
    )


def apply_half(high, low, sides, start, lanes):
    classes = sides[0][0].shape[0]
    rows, depth = high.shape
    count = rows // lanes
    flat = [value for part in sides for value in part]
    begun = list(start or [])

    def kernel(high_ref, low_ref, *refs):
        given, before = refs[: len(flat)], refs[len(flat) : len(flat) + len(begun)]
        outs = refs[len(flat) + len(begun) :]
        at, values = 0, []
        for part in sides:
            value = given[at][...]
            for more in range(1, len(part)):
                value = value + given[at + more][...]
            at += len(part)
            values.append(value)
        value = jnp.concatenate(values, axis=1) if len(values) > 1 else values[0]
        top = value.astype(BF16)
        rest = (value - top.astype(F32)).astype(BF16)
        both = jnp.concatenate([top, rest], axis=0)
        product = lax.dot_general(both, high_ref[...], NT, preferred_element_type=F32)
        total = product[:classes] + product[classes:]
        total = total + lax.dot_general(top, low_ref[...], NT, preferred_element_type=F32)
        for k in range(count):
            piece = total[:, k * lanes : (k + 1) * lanes]
            outs[k][...] = piece + before[k][...] if begun else piece

    return call(
        kernel,
        [of((classes, lanes))] * count,
        [high, low] + flat + begun,
        mib=8,
        flops=6 * classes * rows * depth,
        moved=4 * rows * depth,
        name="apply_half",
    )


def add(lefts, rights, joined=False):
    classes, lanes = lefts[0].shape
    count = len(lefts)
    cover = len(rights) != count

    def kernel(*refs):
        given, outs = refs[: count + len(rights)], refs[count + len(rights) :]
        for k in range(count):
            span = slice(k * lanes, (k + 1) * lanes)
            value = given[k][...] + (given[count][:, span] if cover else given[count + k][...])
            if joined:
                outs[0][:, span] = value
            else:
                outs[k][...] = value

    out = [of((classes, count * lanes))] if joined else [of((classes, lanes))] * count
    return call(kernel, out, list(lefts) + list(rights), mib=4, moved=12 * classes * lanes * count, name="add")


def exchange(parts, axis, orders):
    rounds = len(orders[0])
    for step in range(rounds):
        got = [swap(part, axis, order[step]) for part, order in zip(parts, orders)]
        if step == rounds - 1:
            return [[part, other] for part, other in zip(parts, got)]
        parts = add(parts, got)


def update(current, sides, scalars, start):
    kinds, rows = current.shape
    classes, lanes = sides[0][0].shape
    span = lanes * len(sides)
    count = span // LANES + 1
    last = rows // LANES - 1
    flat = [value for part in sides for value in part]

    def kernel(*refs):
        known = refs[: len(scalars)]
        current_ref = refs[len(scalars)]
        given = refs[len(scalars) + 1 : len(scalars) + 1 + len(flat)]
        out_ref, padded = refs[-2:]
        step = pl.program_id(0)

        @pl.when(step == 0)
        def _():
            edge = jnp.zeros((classes, LANES), F32)
            padded[:, :LANES] = edge
            padded[:, LANES + span : 2 * LANES + span] = edge
            padded[:, 2 * LANES + span :] = edge
            at = 0
            for k, part in enumerate(sides):
                value = given[at][...]
                for more in range(1, len(part)):
                    value = value + given[at + more][...]
                at += len(part)
                padded[:, LANES + k * lanes : LANES + (k + 1) * lanes] = value

        first = start(*known)
        block = jnp.minimum(first // LANES + step, last)
        begin = block * LANES - first + LANES
        aligned = pl.multiple_of(begin // LANES * LANES, LANES)
        value = padded[:, pl.ds(aligned, 2 * LANES)]
        turn = (2 * LANES - begin % LANES) % (2 * LANES)
        value = pltpu.roll(value, turn, 1)[:kinds, :LANES]
        out_ref[...] = current_ref[...] + value

    def at(i, *refs):
        return (0, jnp.minimum(start(*refs) // LANES + i, last))

    whole = pl.BlockSpec((classes, lanes), lambda i, *refs: (0, 0))
    return windowed(
        kernel,
        scalars,
        (count,),
        [pl.BlockSpec((kinds, LANES), at)] + [whole] * len(flat),
        pl.BlockSpec((kinds, LANES), at),
        of((kinds, rows)),
        [current] + flat,
        aliases={len(scalars): 0},
        scratch=[pltpu.VMEM((classes, span + 3 * LANES), F32)],
        mib=6,
        name="update",
    )


def rotations(masks, count):
    return [masks[k % len(masks) :] + masks[: k % len(masks)] for k in range(count)]


def body(features, labels, weights, block_order, block_starts, inverses):
    rows, width = features.shape
    updates, span, stretch_rows = inverses.shape
    kinds = weights.shape[1]
    shards, groups = lax.axis_size("samples"), lax.axis_size("cols")
    piece = stretch_rows // shards
    window = max(piece, LANES)
    classes = up(kinds, 8)
    scale = 1.0 / math.sqrt(rows * shards)
    factor = 2.0 / (width * math.log(2.0))
    lanes = span // 2
    ids = jnp.stack([lax.axis_index("samples"), lax.axis_index("cols")]).astype(I32)
    scalars = [block_order, block_starts, ids]
    turned, weights, labels = features.T, weights.T, labels.reshape(rows // LANES, LANES)

    def place(ids_ref, mask):
        shard = ids_ref[0]
        return shard ^ mask ^ (shard % 2 * (shards // 2))

    def slot(*refs):
        return place(refs[-1], 0) * piece // window

    def inside(*refs):
        return place(refs[-1], 0) * piece % window

    def start(step):
        return lambda order, starts, ids_ref: starts[order[step]]

    def own_start(step):
        return lambda order, starts, ids_ref: starts[order[step]] + ids_ref[1] * piece

    far = list(range(2, shards, 2))

    def gather(step):
        mine = [member_rows(turned, scalars, own_start(step), piece, True)]
        mine += [swap(mine[0], "samples", mask) for mask in far]
        masks = [0] + far + [1 ^ mask for mask in [0] + far]
        pieces = mine + [swap(value, "samples", 1) for value in mine]
        if piece % LANES == 0:
            return assemble(pieces, ids, lambda ids_ref, index: place(ids_ref, masks[index]))
        order = jnp.zeros((shards,), I32).at[place(ids, jnp.array(masks))].set(jnp.arange(shards))
        stacked = jnp.stack(pieces)[order]
        return stacked.transpose(1, 0, 2).reshape(stacked.shape[1], stretch_rows)

    sample_masks = [1 << bit for bit in range(1, shards.bit_length() - 1)]
    col_masks = [(2 << bit) - 1 for bit in range(groups.bit_length() - 1)]
    sample_orders, col_orders = rotations(sample_masks, 2), rotations(col_masks, 2)

    stretches = [gather(step) for step in range(updates)]
    keys, parts, current = prepare(turned, weights, classes)
    members = [member_rows(turned, scalars, start(step), span, False) for step in range(updates - 1)]
    bases = []
    for step in range(updates):
        own = own_terms(weights, labels, scalars, own_start(step), classes, piece, window, inside)
        cuts = [0, rows] if step == 0 else [0, rows // 2, rows]
        base = None
        for first, last in zip(cuts, cuts[1:]):
            base = heavy(keys, parts, stretches[step], base, own, ids, slot, factor, scale, first, last)
        bases.append(base)
    inverse_parts = [split_inverse(inverses, step, ids) for step in range(updates)]
    tiles = {
        (step, later): tile_of(members[step], stretches[later], factor)
        for later in range(1, updates)
        for step in range(later)
    }

    for step in range(updates):
        a, b, send = bases[step]
        summed = add([a, b], [swap(send, "samples", 1)])
        sides = exchange(summed, "samples", sample_orders)
        (residual,) = add([pair[0] for pair in sides], [pair[1] for pair in sides], joined=True)
        other = swap(residual, "samples", 1)
        mine_high, mine_low, other_high, other_low = inverse_parts[step]
        partial = apply_half(mine_high, mine_low, [[residual]], None, lanes)
        partial = apply_half(other_high, other_low, [[other]], partial, lanes)
        sides = exchange(partial, "cols", col_orders)
        for later in range(step + 1, updates):

            def offset(*refs, step=step, later=later):
                return own_start(later)(*refs) - start(step)(*refs)

            *base, delta = correct(
                bases[later], sides, tiles[step, later], scalars, offset, slot, inside, piece, window, scale
            )
            bases[later] = base
            sides = [[delta]]
        current = update(current, sides, scalars, start(step))
    return current.T


def solution(mesh):
    return jax.shard_map(
        body,
        mesh=mesh,
        in_specs=(
            P("samples", None),
            P("samples"),
            P("samples", None),
            P(),
            P(),
            P(None, "samples", "cols"),
        ),
        out_specs=P("samples", None),
        check_vma=False,
    )
```

```python
import math

import jax
import jax.numpy as jnp
from jax import lax
from jax.experimental import pallas as pl
from jax.experimental.pallas import tpu as pltpu
from jax.sharding import PartitionSpec as P

RIDGE = 0.5
F32, BF16, I32 = jnp.float32, jnp.bfloat16, jnp.int32
LANES = 128
VMEM = pl.BlockSpec(memory_space=pltpu.VMEM)
SMEM = pl.BlockSpec(memory_space=pltpu.SMEM)
NT = (((1,), (1,)), ((), ()))


def up(value, unit):
    return -(-value // unit) * unit


def of(shape, kind=F32):
    return jax.ShapeDtypeStruct(shape, kind)


def swap(value, axis, mask):
    size = lax.axis_size(axis)
    return lax.ppermute(value, axis, [(i, i ^ mask) for i in range(size)])


def params(mib, **more):
    return pltpu.CompilerParams(vmem_limit_bytes=mib << 20, **more)


def call(kernel, out, operands, specs=None, mib=8, scratch=(), flops=0, exps=0, moved=0, aliases=None, name=None):
    count = len(operands)
    return pl.pallas_call(
        kernel,
        out_shape=out,
        in_specs=specs or [VMEM] * count,
        out_specs=jax.tree.map(lambda _: VMEM, out),
        scratch_shapes=list(scratch),
        input_output_aliases=aliases or {},
        compiler_params=params(mib),
        cost_estimate=pl.CostEstimate(flops=flops, transcendentals=exps, bytes_accessed=moved),
        name=name,
    )(*operands)


def halves_of_norm(wide):
    value = -0.5 * jnp.sum(wide * wide, axis=0, keepdims=True)
    high = value.astype(BF16).astype(F32)
    middle = (value - high).astype(BF16).astype(F32)
    return high, middle, value - high - middle


def extended(wide, query):
    row = lax.broadcasted_iota(I32, (8, wide.shape[1]), 0)
    tail = jnp.zeros(row.shape, F32)
    first = 3 if query else 0
    for k, part in enumerate(halves_of_norm(wide)):
        tail = jnp.where(row == first + k, part, tail)
        tail = jnp.where(row == 3 - first + k, 1.0, tail)
    return jnp.concatenate([wide, tail], axis=0)


HBM = pl.BlockSpec(memory_space=pltpu.HBM)


def window_at(first, count, total):
    block = jnp.minimum(first // LANES, total // LANES - count)
    return pl.multiple_of(block * LANES, LANES), first - block * LANES


def fetch(source, buffer, sem, start):
    copy = pltpu.make_async_copy(source.at[:, pl.ds(start, buffer.shape[1])], buffer, sem)
    copy.start()
    copy.wait()


def select_query(buffer, shift, count):
    wide = extended(buffer[...].astype(F32), True).astype(BF16)
    shape = (buffer.shape[1], count)
    lane = lax.broadcasted_iota(I32, shape, 0)
    member = lax.broadcasted_iota(I32, shape, 1)
    chosen = jnp.where(lane == member + shift, 1.0, 0.0).astype(BF16)
    return jnp.dot(wide, chosen, preferred_element_type=F32).astype(BF16)


def seen_lanes(count):
    return (up(count, LANES) // LANES + 1) * LANES


def begin(order, starts, ids, turned, updates, piece):
    width, rows = turned.shape
    seen = seen_lanes(piece)

    def kernel(order_hbm, starts_hbm, ids_ref, turned_ref, table_ref, out_ref, order_ref, starts_ref, buffer, sems):
        copies = [
            pltpu.make_async_copy(order_hbm, order_ref, sems.at[0]),
            pltpu.make_async_copy(starts_hbm, starts_ref, sems.at[1]),
        ]
        for copy in copies:
            copy.start()
        for copy in copies:
            copy.wait()
        for step in range(updates):
            first = starts_ref[order_ref[step]]
            table_ref[step] = first
            table_ref[updates + step] = first + ids_ref[1] * piece
        start, shift = window_at(table_ref[updates], seen // LANES, rows)
        fetch(turned_ref, buffer, sems.at[2], start)
        out_ref[...] = select_query(buffer, shift, piece)

    return pl.pallas_call(
        kernel,
        in_specs=[HBM, HBM, SMEM, HBM],
        out_specs=[SMEM, VMEM],
        out_shape=[of((2 * updates,), I32), of((width + 8, piece), BF16)],
        scratch_shapes=[
            pltpu.SMEM(order.shape, I32),
            pltpu.SMEM(starts.shape, I32),
            pltpu.VMEM((width, seen), BF16),
            pltpu.SemaphoreType.DMA((3,)),
        ],
        compiler_params=params(4),
        name="begin",
    )(order, starts, ids, turned)


def query_rows(turned, table, indices, piece):
    width, rows = turned.shape
    seen = seen_lanes(piece)

    def kernel(table_ref, turned_ref, *refs):
        outs, (buffer, sem) = refs[: len(indices)], refs[len(indices) :]
        for index, out_ref in zip(indices, outs):
            start, shift = window_at(table_ref[index], seen // LANES, rows)
            fetch(turned_ref, buffer, sem, start)
            out_ref[...] = select_query(buffer, shift, piece)

    return call(
        kernel,
        [of((width + 8, piece), BF16)] * len(indices),
        [table, turned],
        [SMEM, HBM],
        mib=4,
        scratch=[pltpu.VMEM((width, seen), BF16), pltpu.SemaphoreType.DMA],
        name="query_rows",
    )


def key_rows(turned, table, indices, span):
    width, rows = turned.shape
    seen = seen_lanes(span)

    def kernel(table_ref, turned_ref, *refs):
        outs, (buffer, sem) = refs[: len(indices)], refs[len(indices) :]
        for index, out_ref in zip(indices, outs):
            start, shift = window_at(table_ref[index], seen // LANES, rows)
            fetch(turned_ref, buffer, sem, start)
            wide = extended(buffer[...].astype(F32), False).astype(BF16)
            member = lax.broadcasted_iota(I32, (span, seen), 0)
            lane = lax.broadcasted_iota(I32, (span, seen), 1)
            chosen = jnp.where(lane == member + shift, 1.0, 0.0).astype(BF16)
            rows_of = lax.dot_general(chosen, wide, NT, preferred_element_type=F32)
            out_ref[...] = rows_of.astype(BF16)

    return call(
        kernel,
        [of((span, width + 8), BF16)] * len(indices),
        [table, turned],
        [SMEM, HBM],
        mib=6,
        scratch=[pltpu.VMEM((width, seen), BF16), pltpu.SemaphoreType.DMA],
        name="key_rows",
    )


def own_terms(weights, labels, table, ids, index, classes, piece, window, columns, place):
    kinds, rows = weights.shape
    seen = 2 * LANES
    half, quarter = columns // 2, columns // 4
    last = labels.shape[0] - 1

    def kernel(table_ref, ids_ref, labels_ref, weights_ref, a_ref, b_ref, send_ref, placed, buffer, sem):
        first = table_ref[index]
        start, shift = window_at(first, 2, rows)
        fetch(weights_ref, buffer, sem, start)
        lane_at = place(ids_ref, 0) * piece
        inside = lane_at % window
        turn = (inside - shift + 2 * seen) % seen
        both = pltpu.roll(buffer[...], turn, 1)[:, :LANES]
        block = start // LANES
        lines = [labels_ref[pl.ds(block + k, 1), :] for k in range(2)]
        lines = jnp.broadcast_to(jnp.concatenate(lines, axis=1), (8, seen))
        label = pltpu.roll(lines, turn, 1)[:1, :LANES]
        hot = jnp.where(lax.broadcasted_iota(I32, (kinds, LANES), 0) == label, 1.0, 0.0)
        lane = lax.broadcasted_iota(I32, (kinds, LANES), 1) - inside
        value = jnp.where((lane >= 0) & (lane < piece), hot - RIDGE * both, 0.0)
        placed[...] = jnp.zeros_like(placed)
        placed[:kinds, pl.ds(pl.multiple_of(lane_at // window * window, LANES), LANES)] = value
        a_ref[...] = placed[:, :quarter]
        b_ref[...] = placed[:, quarter:half]
        send_ref[...] = placed[:, half:]

    assert window == LANES
    return call(
        kernel,
        [of((classes, quarter)), of((classes, quarter)), of((classes, half))],
        [table, ids, labels, weights],
        [SMEM, SMEM, VMEM, HBM],
        mib=4,
        scratch=[
            pltpu.VMEM((classes, columns), F32),
            pltpu.VMEM((kinds, seen), F32),
            pltpu.SemaphoreType.DMA,
        ],
        name="own_terms",
    )


def windowed(kernel, scalars, grid, in_specs, out_specs, out, operands, mib=8, name=None):
    return pl.pallas_call(
        kernel,
        grid_spec=pltpu.PrefetchScalarGridSpec(
            num_scalar_prefetch=len(scalars), grid=grid, in_specs=in_specs, out_specs=out_specs
        ),
        out_shape=out,
        compiler_params=params(mib, dimension_semantics=("arbitrary",)),
        cost_estimate=pl.CostEstimate(flops=1 << 20, transcendentals=0, bytes_accessed=1 << 20),
        name=name,
    )(*scalars, *operands)


def prepare(turned, weights, classes, first, last):
    width, rows = turned.shape
    kinds = weights.shape[0]
    depth, block = width + 8, 512
    skip, count = first // block, (last - first) // block

    def kernel(turned_ref, weights_ref, keys_ref, parts_ref):
        wide = extended(turned_ref[...].astype(F32), False)
        keys_ref[...] = wide.T.astype(BF16)
        value = jnp.concatenate([weights_ref[...], jnp.zeros((classes - kinds, block), F32)], axis=0)
        high = value.astype(BF16).astype(F32)
        parts_ref[...] = jnp.concatenate([high, value - high], axis=0).astype(BF16)

    return pl.pallas_call(
        kernel,
        grid=(count,),
        in_specs=[
            pl.BlockSpec((width, block), lambda i: (0, i + skip)),
            pl.BlockSpec((kinds, block), lambda i: (0, i + skip)),
        ],
        out_specs=[
            pl.BlockSpec((block, depth), lambda i: (i, 0)),
            pl.BlockSpec((2 * classes, block), lambda i: (0, i)),
        ],
        out_shape=[of((last - first, depth), BF16), of((2 * classes, last - first), BF16)],
        compiler_params=params(12, dimension_semantics=("arbitrary",)),
        cost_estimate=pl.CostEstimate(flops=1 << 20, transcendentals=0, bytes_accessed=8 << 20),
        name="prepare",
    )(turned, weights)


def copied(weights):
    def kernel(in_ref, out_ref):
        out_ref[...] = in_ref[...]

    kinds, rows = weights.shape
    block = pl.BlockSpec((kinds, 1024), lambda i: (0, i))
    return pl.pallas_call(
        kernel,
        grid=(rows // 1024,),
        in_specs=[block],
        out_specs=block,
        out_shape=of(weights.shape),
        compiler_params=params(4, dimension_semantics=("arbitrary",)),
        name="copied",
    )(weights)


def split_inverse(inverses, index, ids):
    rows, columns = inverses.shape[1:]
    half = columns // 2

    def kernel(ids_ref, *refs):
        for k in range(2):
            value = refs[k][0]
            high = value.astype(BF16)
            refs[2 + 2 * k][...] = high
            refs[3 + 2 * k][...] = (value - high.astype(F32)).astype(BF16)

    def side(k):
        return pl.BlockSpec((1, rows, half), lambda i, ids_ref: (index, 0, (ids_ref[0] + k) % 2))

    return windowed(
        kernel,
        [ids],
        (1,),
        [side(0), side(1)],
        [pl.BlockSpec((rows, half), lambda i, ids_ref: (0, 0))] * 4,
        [of((rows, half), BF16)] * 4,
        [inverses, inverses],
        mib=10,
        name="split_inverse",
    )


def assemble(pieces, ids, place):
    count = len(pieces)
    depth, lanes = pieces[0].shape

    def kernel(ids_ref, *refs):
        for index in range(count):
            start = pl.multiple_of(place(ids_ref, index) * lanes, LANES)
            refs[count][:, pl.ds(start, lanes)] = refs[index][...]

    return call(
        kernel, of((depth, count * lanes), BF16), [ids] + pieces, [SMEM] + [VMEM] * count, mib=4, name="assemble"
    )


def heavy(keys, parts, stretch, base, factor, scale):
    rows, depth = keys.shape
    columns = stretch.shape[1]
    half = columns // 2
    quarter = half // 2
    doubled = parts.shape[0]
    classes = doubled // 2
    block = min(rows, 1024)
    side = block // 2
    wide = min(256, columns)

    def kernel(keys_ref, parts_ref, stretch_ref, a_in, b_in, send_in, a_ref, b_ref, send_ref, total, front, back):
        def fill(panel, start):
            lhs = keys_ref[pl.ds(start, side), :]
            for j in range(columns // wide):
                span = slice(j * wide, (j + 1) * wide)
                inner = jnp.dot(lhs, stretch_ref[:, span], preferred_element_type=F32)
                panel[:, span] = jnp.exp2(inner * factor).astype(BF16)

        def drain(panel, start):
            lhs = parts_ref[:, pl.ds(start, side)]
            for j in range(columns // wide):
                span = slice(j * wide, (j + 1) * wide)
                total[:, span] += jnp.dot(lhs, panel[:, span], preferred_element_type=F32)

        total[...] = jnp.zeros_like(total)
        fill(front, 0)

        def step(i, carry):
            start = pl.multiple_of(i * block, block)
            fill(back, start + side)
            drain(front, start)
            fill(front, start + block)
            drain(back, start + side)
            return carry

        lax.fori_loop(0, rows // block - 1, step, 0)
        fill(back, rows - side)
        drain(front, rows - block)
        drain(back, rows - side)
        spans = [slice(0, quarter), slice(quarter, half), slice(half, columns)]
        for span, given, out in zip(spans, (a_in, b_in, send_in), (a_ref, b_ref, send_ref)):
            out[...] = given[...] - scale * (total[:classes, span] + total[classes:, span])

    return call(
        kernel,
        [of((classes, quarter)), of((classes, quarter)), of((classes, half))],
        [keys, parts, stretch] + list(base),
        mib=16,
        scratch=[
            pltpu.VMEM((doubled, columns), F32),
            pltpu.VMEM((side, columns), BF16),
            pltpu.VMEM((side, columns), BF16),
        ],
        flops=2 * rows * columns * (depth + doubled),
        exps=rows * columns,
        moved=2 * rows * (depth + doubled) + 2 * columns * depth,
        name="heavy",
    )


def tile_of(members, stretch, factor):
    rows, depth = members.shape
    columns = stretch.shape[1]

    def kernel(members_ref, stretch_ref, out_ref):
        inner = jnp.dot(members_ref[...], stretch_ref[...], preferred_element_type=F32)
        out_ref[...] = jnp.exp2(inner * factor).astype(BF16)

    return call(
        kernel,
        of((rows, columns), BF16),
        [members, stretch],
        flops=2 * rows * columns * depth,
        exps=rows * columns,
        moved=2 * rows * (columns + depth) + 2 * columns * depth,
        name="tile",
    )


def correct(base, sides, tile, scalars, offset, slot, inside, piece, window, scale, whole):
    a, b, send = base
    classes, quarter = a.shape
    half = 2 * quarter
    rows, columns = tile.shape
    lanes = rows // len(sides)
    flat = [value for part in sides for value in part]

    def kernel(*refs):
        known = refs[: len(scalars)]
        tile_ref, a_in, b_in, send_in = refs[len(scalars) : len(scalars) + 4]
        given = refs[len(scalars) + 4 : len(scalars) + 4 + len(flat)]
        a_ref, b_ref, send_ref, delta_ref, sums = refs[len(scalars) + 4 + len(flat) :]
        at = 0
        for k, part in enumerate(sides):
            value = given[at][...]
            for more in range(1, len(part)):
                value = value + given[at + more][...]
            at += len(part)
            delta_ref[:, k * lanes : (k + 1) * lanes] = value
        delta = delta_ref[...]
        high = delta.astype(BF16)
        rest = delta - high.astype(F32)
        middle = rest.astype(BF16)
        low = (rest - middle.astype(F32)).astype(BF16)
        both = jnp.concatenate([high, middle], axis=0)
        product = jnp.dot(both, tile_ref[...], preferred_element_type=F32)
        sums[...] = -scale * (product[:classes] + product[classes:])
        row = lax.broadcasted_iota(I32, (rows, window), 0)
        lane = lax.broadcasted_iota(I32, (rows, window), 1) - inside(*known)
        match = (row == lane + offset(*known)) & (lane >= 0) & (lane < piece)
        chosen = jnp.where(match, 1.0, 0.0).astype(BF16)
        picked = jnp.dot(jnp.concatenate([both, low], axis=0), chosen, preferred_element_type=F32)
        picked = picked[:classes] + picked[classes : 2 * classes] + picked[2 * classes :]
        span = pl.ds(pl.multiple_of(slot(*known) * window, LANES), window)
        sums[:, span] = sums[:, span] - RIDGE * picked
        a_ref[...] = a_in[...] + sums[:, :quarter]
        b_ref[...] = b_in[...] + sums[:, quarter:half]
        send_ref[...] = send_in[...] + sums[:, half:]

    return call(
        kernel,
        [of(a.shape), of(b.shape), of(send.shape), of((classes, rows))],
        list(scalars) + [tile, a, b, send] + flat,
        [SMEM] * len(scalars) + [VMEM] * (4 + len(flat)),
        mib=10,
        scratch=[pltpu.VMEM((classes, columns), F32)],
        flops=4 * classes * rows * columns,
        moved=2 * rows * columns,
        name="correct",
    )


def apply_half(high, low, sides, start, lanes):
    classes = sides[0][0].shape[0]
    rows, depth = high.shape
    count = rows // lanes
    flat = [value for part in sides for value in part]
    begun = list(start or [])

    def kernel(high_ref, low_ref, *refs):
        given, before = refs[: len(flat)], refs[len(flat) : len(flat) + len(begun)]
        outs = refs[len(flat) + len(begun) :]
        at, values = 0, []
        for part in sides:
            value = given[at][...]
            for more in range(1, len(part)):
                value = value + given[at + more][...]
            at += len(part)
            values.append(value)
        value = jnp.concatenate(values, axis=1) if len(values) > 1 else values[0]
        top = value.astype(BF16)
        rest = (value - top.astype(F32)).astype(BF16)
        both = jnp.concatenate([top, rest], axis=0)
        product = lax.dot_general(both, high_ref[...], NT, preferred_element_type=F32)
        total = product[:classes] + product[classes:]
        total = total + lax.dot_general(top, low_ref[...], NT, preferred_element_type=F32)
        for k in range(count):
            piece = total[:, k * lanes : (k + 1) * lanes]
            outs[k][...] = piece + before[k][...] if begun else piece

    return call(
        kernel,
        [of((classes, lanes))] * count,
        [high, low] + flat + begun,
        mib=8,
        flops=6 * classes * rows * depth,
        moved=4 * rows * depth,
        name="apply_half",
    )


def add(lefts, rights, joined=False):
    classes, lanes = lefts[0].shape
    count = len(lefts)
    cover = len(rights) != count

    def kernel(*refs):
        given, outs = refs[: count + len(rights)], refs[count + len(rights) :]
        for k in range(count):
            span = slice(k * lanes, (k + 1) * lanes)
            value = given[k][...] + (given[count][:, span] if cover else given[count + k][...])
            if joined:
                outs[0][:, span] = value
            else:
                outs[k][...] = value

    out = [of((classes, count * lanes))] if joined else [of((classes, lanes))] * count
    return call(kernel, out, list(lefts) + list(rights), mib=4, moved=12 * classes * lanes * count, name="add")


def peek(current, table, index, span):
    kinds, rows = current.shape
    seen = seen_lanes(span)

    def kernel(table_ref, current_ref, out_ref, sem):
        start, unused = window_at(table_ref[index], seen // LANES, rows)
        fetch(current_ref, out_ref, sem, start)

    return call(
        kernel, of((kinds, seen)), [table, current], [SMEM, HBM], mib=3, scratch=[pltpu.SemaphoreType.DMA], name="peek"
    )


def update(current, before, sides, table, index):
    kinds, rows = current.shape
    classes, lanes = sides[0][0].shape
    span = lanes * len(sides)
    seen = seen_lanes(span)
    flat = [value for part in sides for value in part]

    def kernel(table_ref, current_ref, before_ref, *refs):
        given, (out_ref, buffer, sem) = refs[: len(flat)], refs[len(flat) :]
        at, values = 0, []
        for part in sides:
            value = given[at][...]
            for more in range(1, len(part)):
                value = value + given[at + more][...]
            at += len(part)
            values.append(value)
        start, shift = window_at(table_ref[index], seen // LANES, rows)
        value = jnp.concatenate(values + [jnp.zeros((classes, seen - span), F32)], axis=1)
        buffer[...] = before_ref[...] + pltpu.roll(value, shift, 1)[:kinds]
        copy = pltpu.make_async_copy(buffer, out_ref.at[:, pl.ds(start, seen)], sem)
        copy.start()
        copy.wait()

    return pl.pallas_call(
        kernel,
        in_specs=[SMEM, HBM] + [VMEM] * (1 + len(flat)),
        out_specs=HBM,
        out_shape=of((kinds, rows)),
        input_output_aliases={1: 0},
        scratch_shapes=[pltpu.VMEM((kinds, seen), F32), pltpu.SemaphoreType.DMA],
        compiler_params=params(4),
        name="update",
    )(table, current, before, *flat)


def rotations(masks, count):
    return [masks[k % len(masks) :] + masks[: k % len(masks)] for k in range(count)]


class Windows:
    def __init__(self):
        self.have, self.queue = {}, []

    def later(self, key, cost, anchor, needs, run, loose=False):
        self.queue.append((key, cost, anchor, needs, run, loose))

    def chosen(self, budget, forced):
        picked, known = [], set(self.have)
        for entry in list(self.queue):
            key, cost, anchor, needs, run, loose = entry
            if not set(needs) <= known:
                continue
            if key in forced or cost <= budget:
                budget -= cost
                picked.append(entry)
                known.add(key)
                self.queue.remove(entry)
        return picked

    def around(self, values, transfer, budget, forced=()):
        picked = self.chosen(budget, forced)
        anchors = [entry[2] for entry in picked if entry[2] in self.have]
        values, tied = lax.optimization_barrier((values, {key: self.have[key] for key in anchors}))
        self.have.update(tied)
        got = transfer(values)
        for key, cost, anchor, needs, run, loose in picked:
            self.have[key] = run()
        held = {entry[0]: self.have[entry[0]] for entry in picked if not entry[5]}
        (values, got), held = lax.optimization_barrier(((values, got), held))
        self.have.update(held)
        return values, got


def body(features, labels, weights, block_order, block_starts, inverses):
    rows, width = features.shape
    updates, span, stretch_rows = inverses.shape
    kinds = weights.shape[1]
    shards, groups = lax.axis_size("samples"), lax.axis_size("cols")
    piece = stretch_rows // shards
    window = max(piece, LANES)
    classes = up(kinds, 8)
    scale = 1.0 / math.sqrt(rows * shards)
    factor = 2.0 / (width * math.log(2.0))
    lanes = span // 2
    ids = jnp.stack([lax.axis_index("samples"), lax.axis_index("cols")]).astype(I32)
    turned, weights, labels = features.T, weights.T, labels.reshape(rows // LANES, LANES)

    def place(ids_ref, mask):
        shard = ids_ref[0]
        return shard ^ mask ^ (shard % 2 * (shards // 2))

    def slot(*refs):
        return place(refs[-1], 0) * piece // window

    def inside(*refs):
        return place(refs[-1], 0) * piece % window

    far = list(range(2, shards, 2))
    masks = [0] + far + [1 ^ mask for mask in [0] + far]
    sample_masks = [1 << bit for bit in range(1, shards.bit_length() - 1)]
    col_masks = [(2 << bit) - 1 for bit in range(groups.bit_length() - 1)]
    sample_orders, col_orders = rotations(sample_masks, 2), rotations(col_masks, 2)

    def spread(mine):
        return [mine] + [swap(mine, "samples", mask) for mask in far]

    def joined(mine, other):
        pieces = mine + other
        if piece % LANES == 0:
            return assemble(pieces, ids, lambda ids_ref, index: place(ids_ref, masks[index]))
        order = jnp.zeros((shards,), I32).at[place(ids, jnp.array(masks))].set(jnp.arange(shards))
        stacked = jnp.stack(pieces)[order]
        return stacked.transpose(1, 0, 2).reshape(stacked.shape[1], stretch_rows)

    def partner(values):
        return [swap(value, "samples", 1) for value in values]

    flow = Windows()
    have = flow.have
    table, query = begin(block_order, block_starts, ids, turned, updates, piece)
    have["table"], have["turned"], have["weights"], have["inverses"] = table, turned, weights, inverses
    later_steps = list(range(1, updates))
    middle = rows // 2

    def queue_own(step):
        flow.later(
            f"base{step}",
            0.8,
            "table",
            ["table"],
            lambda: own_terms(
                weights, labels, have["table"], ids, updates + step, classes, piece, window, stretch_rows, place
            ),
        )

    def queue_split(step):
        flow.later(
            f"inverse{step}", 1.0, "ids", [], lambda: split_inverse(inverses, step, have["ids"])
        )

    def queue_heavy(step):
        for k in range(2):

            def run(k=k):
                have[f"base{step}"] = heavy(*have[f"keys{k}"], have[f"stretch{step}"], have[f"base{step}"], factor, scale)
                return have[f"base{step}"][0]

            needs = [f"stretch{step}", f"base{step}", f"keys{k}"] + ([f"heavy{step}.0"] if k else [])
            flow.later(f"heavy{step}.{k}", 4.3, f"base{step}", needs, run)

    def queue_tile(step, later):
        flow.later(
            f"tile{step}.{later}",
            0.8,
            f"member{step}",
            [f"member{step}", f"stretch{later}"],
            lambda: tile_of(have[f"member{step}"], have[f"stretch{later}"], factor),
        )

    def correction(step, later, sides):
        def offset(table_ref, ids_ref):
            return table_ref[updates + later] - table_ref[step]

        *base, delta = correct(
            have[f"base{later}"],
            sides,
            have[f"tile{step}.{later}"],
            [have["table"], ids],
            offset,
            slot,
            inside,
            piece,
            window,
            scale,
            len(sides) > 1,
        )
        have[f"base{later}"] = base
        return delta

    def queue_correction(step, later):
        def run():
            correction(step, later, [[have[f"delta{step}"]]])
            return have[f"base{later}"][0]

        flow.later(
            f"correct{step}.{later}",
            1.4,
            f"delta{step}",
            [f"delta{step}", f"tile{step}.{later}", f"heavy{later}.1"],
            run,
        )

    def queue_stretch(step):
        flow.later(f"far{step}", 1.0, f"query{step}", [f"query{step}"], lambda: spread(have[f"query{step}"]), True)

    def queue_join(step):
        flow.later(
            f"stretch{step}", 2.0, f"far{step}", [f"far{step}"], lambda: joined(have[f"far{step}"], partner(have[f"far{step}"]))
        )

    def queue_update(step):
        def run():
            before = peek(have["current"], have["table"], step, span)
            have["current"] = update(have["current"], before, [[have[f"delta{step}"]]], have["table"], step)
            return have["current"]

        flow.later(f"update{step}", 2.5, f"delta{step}", [f"delta{step}", "current"], run)

    have["ids"] = ids
    for k in range(2):
        flow.later(
            f"keys{k}", 2.5, "table", [], lambda k=k: prepare(turned, weights, classes, k * middle, (k + 1) * middle)
        )
    queue_own(0)
    table_steps = [updates + step for step in later_steps]

    def run_queries():
        values = query_rows(turned, have["table"], table_steps, piece)
        for step, value in zip(later_steps, values):
            have[f"query{step}"] = value
        return values[-1]

    flow.later("queries", 2.0, "table", ["table"], run_queries)
    query, pieces = flow.around(query, spread, 100.0)

    def run_members():
        values = key_rows(turned, have["table"], list(range(updates - 1)), span)
        for step, value in enumerate(values):
            have[f"member{step}"] = value
        return values[-1]

    queue_split(0)
    for step in later_steps[:1]:
        queue_stretch(step)
    pieces, others = flow.around(pieces, partner, 1.0)
    have["stretch0"] = joined(pieces, others)
    for step in later_steps[:1]:
        flow.queue = [entry for entry in flow.queue if entry[0] != f"far{step}"]
        have["stretch0"], have[f"query{step}"] = lax.optimization_barrier((have["stretch0"], have[f"query{step}"]))
        have[f"far{step}"] = spread(have[f"query{step}"])
    for k in range(2):
        have["base0"] = heavy(*have[f"keys{k}"], have["stretch0"], have["base0"], factor, scale)

    flow.later("members", 3.0, "table", ["table"], run_members)
    for step in later_steps:
        flow.later("current", 2.0, "weights", [], lambda: copied(have["weights"])) if step == 1 else None
        queue_own(step)
        queue_join(step)
        queue_heavy(step)
        for before in range(step):
            queue_tile(before, step)
            if before < step - 1:
                queue_correction(before, step)
        queue_split(step)
    for step in range(updates - 1):
        queue_update(step)

    for step in range(updates):
        a, b, send = have[f"base{step}"]
        follow = step + 1
        forced = [f"stretch{follow}", f"base{follow}"]
        (a, b, send), got = flow.around((a, b, send), lambda values: swap(values[2], "samples", 1), 1.0, forced)
        parts = add([a, b], [got])
        for turn in range(len(sample_orders[0])):
            if turn:
                parts = add(parts, got)
            parts, got = flow.around(
                parts,
                lambda values: [swap(value, "samples", order[turn]) for value, order in zip(values, sample_orders)],
                5.5,
            )
        (residual,) = add(parts, got, joined=True)
        mine_high, mine_low, other_high, other_low = have[f"inverse{step}"]
        other = swap(residual, "samples", 1)
        partial = apply_half(mine_high, mine_low, [[residual]], None, lanes)
        parts = apply_half(other_high, other_low, [[other]], partial, lanes)
        if step == 0:
            for later in later_steps[1:]:
                queue_stretch(later)
        rounds = len(col_orders[0])
        for turn in range(rounds):
            if turn:
                parts = add(parts, got)
            forced = []
            if step == 0:
                forced = [f"far{later}" for later in later_steps[1:]]
            if turn == rounds - 1 and follow < updates:
                forced += [entry[0] for entry in flow.queue if entry[0].endswith(f".{follow}")]
                forced += [f"heavy{follow}.{k}" for k in range(2)] + [f"inverse{follow}", "members"]
            parts, got = flow.around(
                parts,
                lambda values: [swap(value, "cols", order[turn]) for value, order in zip(values, col_orders)],
                7.0,
                forced,
            )
        sides = [[part, other] for part, other in zip(parts, got)]
        if follow < updates:
            have[f"delta{step}"] = correction(step, follow, sides)
        elif follow == updates:
            current = update(have["current"], have["before"], sides, have["table"], step)
        if follow == updates - 1:
            flow.later(
                "before",
                1.5,
                "current",
                [f"update{before}" for before in range(updates - 1)],
                lambda: peek(have["current"], have["table"], updates - 1, span),
            )
    return current.T


def solution(mesh):
    return jax.shard_map(
        body,
        mesh=mesh,
        in_specs=(
            P("samples", None),
            P("samples"),
            P("samples", None),
            P(),
            P(),
            P(None, "samples", "cols"),
        ),
        out_specs=P("samples", None),
        check_vma=False,
    )
```

```python
import math

import jax
import jax.numpy as jnp
from jax import lax
from jax.experimental import pallas as pl
from jax.experimental.pallas import tpu as pltpu
from jax.sharding import PartitionSpec as P

RIDGE = 0.5
F32, BF16, I32 = jnp.float32, jnp.bfloat16, jnp.int32
LANES = 128
VMEM = pl.BlockSpec(memory_space=pltpu.VMEM)
SMEM = pl.BlockSpec(memory_space=pltpu.SMEM)
NT = (((1,), (1,)), ((), ()))


def up(value, unit):
    return -(-value // unit) * unit


def of(shape, kind=F32):
    return jax.ShapeDtypeStruct(shape, kind)


def swap(value, axis, mask):
    size = lax.axis_size(axis)
    return lax.ppermute(value, axis, [(i, i ^ mask) for i in range(size)])


def params(mib, **more):
    return pltpu.CompilerParams(vmem_limit_bytes=mib << 20, **more)


def call(kernel, out, operands, specs=None, mib=8, scratch=(), flops=0, exps=0, moved=0, aliases=None, name=None):
    count = len(operands)
    return pl.pallas_call(
        kernel,
        out_shape=out,
        in_specs=specs or [VMEM] * count,
        out_specs=jax.tree.map(lambda _: VMEM, out),
        scratch_shapes=list(scratch),
        input_output_aliases=aliases or {},
        compiler_params=params(mib),
        cost_estimate=pl.CostEstimate(flops=flops, transcendentals=exps, bytes_accessed=moved),
        name=name,
    )(*operands)


def halves_of_norm(wide):
    value = -0.5 * jnp.sum(wide * wide, axis=0, keepdims=True)
    high = value.astype(BF16).astype(F32)
    middle = (value - high).astype(BF16).astype(F32)
    return high, middle, value - high - middle


def extended(wide, query):
    row = lax.broadcasted_iota(I32, (8, wide.shape[1]), 0)
    tail = jnp.zeros(row.shape, F32)
    first = 3 if query else 0
    for k, part in enumerate(halves_of_norm(wide)):
        tail = jnp.where(row == first + k, part, tail)
        tail = jnp.where(row == 3 - first + k, 1.0, tail)
    return jnp.concatenate([wide, tail], axis=0)


HBM = pl.BlockSpec(memory_space=pltpu.HBM)


def window_at(first, count, total):
    block = jnp.minimum(first // LANES, total // LANES - count)
    return pl.multiple_of(block * LANES, LANES), first - block * LANES


def fetch(source, buffer, sem, start):
    copy = pltpu.make_async_copy(source.at[:, pl.ds(start, buffer.shape[1])], buffer, sem)
    copy.start()
    copy.wait()


def select_query(buffer, shift, count):
    wide = extended(buffer[...].astype(F32), True).astype(BF16)
    shape = (buffer.shape[1], count)
    lane = lax.broadcasted_iota(I32, shape, 0)
    member = lax.broadcasted_iota(I32, shape, 1)
    chosen = jnp.where(lane == member + shift, 1.0, 0.0).astype(BF16)
    return jnp.dot(wide, chosen, preferred_element_type=F32).astype(BF16)


def seen_lanes(count):
    return (up(count, LANES) // LANES + 1) * LANES


def begin(order, starts, ids, turned, updates, piece):
    width, rows = turned.shape
    seen = seen_lanes(piece)

    def kernel(order_hbm, starts_hbm, ids_ref, turned_ref, table_ref, out_ref, order_ref, starts_ref, buffer, sems):
        copies = [
            pltpu.make_async_copy(order_hbm, order_ref, sems.at[0]),
            pltpu.make_async_copy(starts_hbm, starts_ref, sems.at[1]),
        ]
        for copy in copies:
            copy.start()
        for copy in copies:
            copy.wait()
        for step in range(updates):
            first = starts_ref[order_ref[step]]
            table_ref[step] = first
            table_ref[updates + step] = first + ids_ref[1] * piece
        start, shift = window_at(table_ref[updates], seen // LANES, rows)
        fetch(turned_ref, buffer, sems.at[2], start)
        out_ref[...] = select_query(buffer, shift, piece)

    return pl.pallas_call(
        kernel,
        in_specs=[HBM, HBM, SMEM, HBM],
        out_specs=[SMEM, VMEM],
        out_shape=[of((2 * updates,), I32), of((width + 8, piece), BF16)],
        scratch_shapes=[
            pltpu.SMEM(order.shape, I32),
            pltpu.SMEM(starts.shape, I32),
            pltpu.VMEM((width, seen), BF16),
            pltpu.SemaphoreType.DMA((3,)),
        ],
        compiler_params=params(60),
        name="begin",
    )(order, starts, ids, turned)


def query_rows(turned, table, sets, piece):
    width, rows = turned.shape
    seen = seen_lanes(piece)

    def kernel(table_ref, turned_ref, *refs):
        outs, (buffer, sem) = refs[: len(sets)], refs[len(sets) :]
        for indices, out_ref in zip(sets, outs):
            for k, index in enumerate(indices):
                start, shift = window_at(table_ref[index], seen // LANES, rows)
                fetch(turned_ref, buffer, sem, start)
                out_ref[:, k * piece : (k + 1) * piece] = select_query(buffer, shift, piece)

    return call(
        kernel,
        [of((width + 8, len(indices) * piece), BF16) for indices in sets],
        [table, turned],
        [SMEM, HBM],
        mib=4,
        scratch=[pltpu.VMEM((width, seen), BF16), pltpu.SemaphoreType.DMA],
        name="query_rows",
    )


def key_rows(turned, table, count, span):
    width, rows = turned.shape
    seen = seen_lanes(span)

    def kernel(table_ref, turned_ref, out_ref, buffer, sem):
        def step(index, carry):
            start, shift = window_at(table_ref[index], seen // LANES, rows)
            fetch(turned_ref, buffer, sem, start)
            wide = extended(buffer[...].astype(F32), False).astype(BF16)
            member = lax.broadcasted_iota(I32, (span, seen), 0)
            lane = lax.broadcasted_iota(I32, (span, seen), 1)
            chosen = jnp.where(lane == member + shift, 1.0, 0.0).astype(BF16)
            rows_of = lax.dot_general(chosen, wide, NT, preferred_element_type=F32)
            out_ref[pl.ds(index, 1)] = rows_of.astype(BF16)[None]
            return carry

        lax.fori_loop(0, count, step, 0)

    return call(
        kernel,
        of((count, span, width + 8), BF16),
        [table, turned],
        [SMEM, HBM],
        mib=8,
        scratch=[pltpu.VMEM((width, seen), BF16), pltpu.SemaphoreType.DMA],
        name="key_rows",
    )


def own_terms(weights, labels, table, ids, index, classes, piece, window, columns, place):
    kinds, rows = weights.shape
    seen = 2 * LANES
    half, quarter = columns // 2, columns // 4
    last = labels.shape[0] - 1

    def kernel(table_ref, ids_ref, labels_ref, weights_ref, a_ref, b_ref, send_ref, placed, buffer, sem):
        first = table_ref[index]
        start, shift = window_at(first, 2, rows)
        fetch(weights_ref, buffer, sem, start)
        lane_at = place(ids_ref, 0) * piece
        inside = lane_at % window
        turn = (inside - shift + 2 * seen) % seen
        both = pltpu.roll(buffer[...], turn, 1)[:, :LANES]
        block = start // LANES
        lines = [labels_ref[pl.ds(block + k, 1), :] for k in range(2)]
        lines = jnp.broadcast_to(jnp.concatenate(lines, axis=1), (8, seen))
        label = pltpu.roll(lines, turn, 1)[:1, :LANES]
        hot = jnp.where(lax.broadcasted_iota(I32, (kinds, LANES), 0) == label, 1.0, 0.0)
        lane = lax.broadcasted_iota(I32, (kinds, LANES), 1) - inside
        value = jnp.where((lane >= 0) & (lane < piece), hot - RIDGE * both, 0.0)
        placed[...] = jnp.zeros_like(placed)
        placed[:kinds, pl.ds(pl.multiple_of(lane_at // window * window, LANES), LANES)] = value
        a_ref[...] = placed[:, :quarter]
        b_ref[...] = placed[:, quarter:half]
        send_ref[...] = placed[:, half:]

    assert window == LANES
    return call(
        kernel,
        [of((classes, quarter)), of((classes, quarter)), of((classes, half))],
        [table, ids, labels, weights],
        [SMEM, SMEM, VMEM, HBM],
        mib=4,
        scratch=[
            pltpu.VMEM((classes, columns), F32),
            pltpu.VMEM((kinds, seen), F32),
            pltpu.SemaphoreType.DMA,
        ],
        name="own_terms",
    )


def windowed(kernel, scalars, grid, in_specs, out_specs, out, operands, mib=8, name=None):
    return pl.pallas_call(
        kernel,
        grid_spec=pltpu.PrefetchScalarGridSpec(
            num_scalar_prefetch=len(scalars), grid=grid, in_specs=in_specs, out_specs=out_specs
        ),
        out_shape=out,
        compiler_params=params(mib, dimension_semantics=("arbitrary",)),
        cost_estimate=pl.CostEstimate(flops=1 << 20, transcendentals=0, bytes_accessed=1 << 20),
        name=name,
    )(*scalars, *operands)


def prepare(turned, weights, classes):
    width, rows = turned.shape
    kinds = weights.shape[0]
    depth, block = width + 8, 512

    def kernel(turned_ref, weights_ref, keys_ref, parts_ref):
        wide = extended(turned_ref[...].astype(F32), False)
        keys_ref[...] = wide.T.astype(BF16)
        value = jnp.concatenate([weights_ref[...], jnp.zeros((classes - kinds, block), F32)], axis=0)
        high = value.astype(BF16).astype(F32)
        parts_ref[...] = jnp.concatenate([high, value - high], axis=0).astype(BF16)

    return pl.pallas_call(
        kernel,
        grid=(rows // block,),
        in_specs=[
            pl.BlockSpec((width, block), lambda i: (0, i)),
            pl.BlockSpec((kinds, block), lambda i: (0, i)),
        ],
        out_specs=[
            pl.BlockSpec((block, depth), lambda i: (i, 0)),
            pl.BlockSpec((2 * classes, block), lambda i: (0, i)),
        ],
        out_shape=[of((rows, depth), BF16), of((2 * classes, rows), BF16)],
        compiler_params=params(12, dimension_semantics=("arbitrary",)),
        cost_estimate=pl.CostEstimate(flops=1 << 20, transcendentals=0, bytes_accessed=8 << 20),
        name="prepare",
    )(turned, weights)


def split_inverse(inverses, index, ids):
    rows, columns = inverses.shape[1:]
    half = columns // 2
    block = min(rows, 128)

    def kernel(ids_ref, *refs):
        def step(i, carry):
            at = pl.ds(pl.multiple_of(i * block, block), block)
            for k in range(2):
                value = refs[k][0, at, :]
                high = value.astype(BF16)
                refs[2 + 2 * k][at, :] = high
                refs[3 + 2 * k][at, :] = (value - high.astype(F32)).astype(BF16)
            return carry

        lax.fori_loop(0, rows // block, step, 0)

    def side(k):
        return pl.BlockSpec((1, rows, half), lambda i, ids_ref: (index, 0, (ids_ref[0] + k) % 2))

    return windowed(
        kernel,
        [ids],
        (1,),
        [side(0), side(1)],
        [pl.BlockSpec((rows, half), lambda i, ids_ref: (0, 0))] * 4,
        [of((rows, half), BF16)] * 4,
        [inverses, inverses],
        mib=10,
        name="split_inverse",
    )


def assemble(pieces, ids, place, sets, lanes):
    count = len(pieces)
    depth = pieces[0].shape[0]

    def kernel(ids_ref, *refs):
        for index in range(count):
            start = pl.multiple_of(place(ids_ref, index) * lanes, LANES)
            for k in range(sets):
                refs[count + k][:, pl.ds(start, lanes)] = refs[index][:, k * lanes : (k + 1) * lanes]

    out = [of((depth, count * lanes), BF16)] * sets
    return call(kernel, out, [ids] + pieces, [SMEM] + [VMEM] * count, mib=6, name="assemble")


def heavy(keys, parts, stretch, base, factor, scale, first, last):
    rows, depth = last - first, keys.shape[1]
    columns = stretch.shape[1]
    half = columns // 2
    quarter = half // 2
    doubled = parts.shape[0]
    classes = doubled // 2
    block = min(rows, 1024)
    side = block // 2
    wide = min(256, columns)

    def kernel(keys_ref, parts_ref, stretch_ref, a_in, b_in, send_in, a_ref, b_ref, send_ref, total, front, back):
        def fill(panel, start):
            lhs = keys_ref[pl.ds(first + start, side), :]
            for j in range(columns // wide):
                span = slice(j * wide, (j + 1) * wide)
                inner = jnp.dot(lhs, stretch_ref[:, span], preferred_element_type=F32)
                panel[:, span] = jnp.exp2(inner * factor).astype(BF16)

        def drain(panel, start):
            lhs = parts_ref[:, pl.ds(first + start, side)]
            for j in range(columns // wide):
                span = slice(j * wide, (j + 1) * wide)
                total[:, span] += jnp.dot(lhs, panel[:, span], preferred_element_type=F32)

        total[...] = jnp.zeros_like(total)
        fill(front, 0)

        def step(i, carry):
            start = pl.multiple_of(i * block, block)
            fill(back, start + side)
            drain(front, start)
            fill(front, start + block)
            drain(back, start + side)
            return carry

        lax.fori_loop(0, rows // block - 1, step, 0)
        fill(back, rows - side)
        drain(front, rows - block)
        drain(back, rows - side)
        spans = [slice(0, quarter), slice(quarter, half), slice(half, columns)]
        for span, given, out in zip(spans, (a_in, b_in, send_in), (a_ref, b_ref, send_ref)):
            out[...] = given[...] - scale * (total[:classes, span] + total[classes:, span])

    return call(
        kernel,
        [of((classes, quarter)), of((classes, quarter)), of((classes, half))],
        [keys, parts, stretch] + list(base),
        mib=16,
        scratch=[
            pltpu.VMEM((doubled, columns), F32),
            pltpu.VMEM((side, columns), BF16),
            pltpu.VMEM((side, columns), BF16),
        ],
        flops=2 * rows * columns * (depth + doubled),
        exps=rows * columns,
        moved=2 * rows * (depth + doubled) + 2 * columns * depth,
        name="heavy",
    )


def tile_of(members, index, stretch, factor):
    rows, depth = members.shape[1:]
    columns = stretch.shape[1]
    wide = min(512, columns)

    def kernel(members_ref, stretch_ref, out_ref):
        def step(j, carry):
            span = pl.ds(pl.multiple_of(j * wide, wide), wide)
            inner = jnp.dot(members_ref[index], stretch_ref[:, span], preferred_element_type=F32)
            out_ref[:, span] = jnp.exp2(inner * factor).astype(BF16)
            return carry

        lax.fori_loop(0, columns // wide, step, 0)

    return call(
        kernel,
        of((rows, columns), BF16),
        [members, stretch],
        flops=2 * rows * columns * depth,
        exps=rows * columns,
        moved=2 * rows * (columns + depth) + 2 * columns * depth,
        name="tile",
    )


class Sides:
    def __init__(self, parts, placed):
        self.parts, self.placed = parts, placed
        self.flat = [value for part in parts for value in part]
        self.lanes = parts[0][0].shape[1]
        self.span = self.lanes * len(parts)

    def fill(self, given, out, ids_ref, base=0):
        at = 0
        for k, part in enumerate(self.parts):
            value = given[at][...]
            for more in range(1, len(part)):
                value = value + given[at + more][...]
            at += len(part)
            if self.placed:
                out[:, pl.ds(pl.multiple_of((ids_ref[1] ^ k) * self.lanes, LANES), self.lanes)] = value
            else:
                out[:, k * self.lanes : (k + 1) * self.lanes] = value


def correct(base, sides, tile, scalars, offset, slot, inside, piece, window, scale):
    a, b, send = base
    classes, quarter = a.shape
    half = 2 * quarter
    rows, columns = tile.shape
    flat = sides.flat

    def kernel(*refs):
        known = refs[: len(scalars)]
        tile_ref, a_in, b_in, send_in = refs[len(scalars) : len(scalars) + 4]
        given = refs[len(scalars) + 4 : len(scalars) + 4 + len(flat)]
        a_ref, b_ref, send_ref, delta_ref, sums = refs[len(scalars) + 4 + len(flat) :]
        sides.fill(given, delta_ref, known[-1])
        delta = delta_ref[...]
        high = delta.astype(BF16)
        rest = delta - high.astype(F32)
        middle = rest.astype(BF16)
        low = (rest - middle.astype(F32)).astype(BF16)
        both = jnp.concatenate([high, middle], axis=0)
        product = jnp.dot(both, tile_ref[...], preferred_element_type=F32)
        sums[...] = -scale * (product[:classes] + product[classes:])
        row = lax.broadcasted_iota(I32, (rows, window), 0)
        lane = lax.broadcasted_iota(I32, (rows, window), 1) - inside(*known)
        match = (row == lane + offset(*known)) & (lane >= 0) & (lane < piece)
        chosen = jnp.where(match, 1.0, 0.0).astype(BF16)
        picked = jnp.dot(jnp.concatenate([both, low], axis=0), chosen, preferred_element_type=F32)
        picked = picked[:classes] + picked[classes : 2 * classes] + picked[2 * classes :]
        span = pl.ds(pl.multiple_of(slot(*known) * window, LANES), window)
        sums[:, span] = sums[:, span] - RIDGE * picked
        a_ref[...] = a_in[...] + sums[:, :quarter]
        b_ref[...] = b_in[...] + sums[:, quarter:half]
        send_ref[...] = send_in[...] + sums[:, half:]

    return call(
        kernel,
        [of(a.shape), of(b.shape), of(send.shape), of((classes, rows))],
        list(scalars) + [tile, a, b, send] + flat,
        [SMEM] * len(scalars) + [VMEM] * (4 + len(flat)),
        mib=10,
        scratch=[pltpu.VMEM((classes, columns), F32)],
        flops=4 * classes * rows * columns,
        moved=2 * rows * columns,
        name="correct",
    )


def apply_half(high, low, sides, start, lanes, ids, placed):
    classes = sides[0][0].shape[0]
    rows, depth = high.shape
    count = rows // lanes
    flat = [value for part in sides for value in part]
    begun = list(start or [])

    def kernel(ids_ref, high_ref, low_ref, *refs):
        given, before = refs[: len(flat)], refs[len(flat) : len(flat) + len(begun)]
        outs, whole = refs[len(flat) + len(begun) : -1], refs[-1]
        at, values = 0, []
        for part in sides:
            value = given[at][...]
            for more in range(1, len(part)):
                value = value + given[at + more][...]
            at += len(part)
            values.append(value)
        value = jnp.concatenate(values, axis=1) if len(values) > 1 else values[0]
        top = value.astype(BF16)
        rest = (value - top.astype(F32)).astype(BF16)
        both = jnp.concatenate([top, rest], axis=0)
        product = lax.dot_general(both, high_ref[...], NT, preferred_element_type=F32)
        total = product[:classes] + product[classes:]
        total = total + lax.dot_general(top, low_ref[...], NT, preferred_element_type=F32)
        if begun:
            total = total + before[0][...]
        if placed:
            whole[...] = total
        for k in range(count):
            if placed:
                at = pl.ds(pl.multiple_of((ids_ref[1] ^ k) * lanes, LANES), lanes)
                outs[k][...] = whole[:, at]
            else:
                outs[k][...] = total[:, k * lanes : (k + 1) * lanes]

    return call(
        kernel,
        [of((classes, lanes))] * count,
        [ids, high, low] + flat + begun,
        [SMEM] + [VMEM] * (2 + len(flat) + len(begun)),
        mib=8,
        scratch=[pltpu.VMEM((classes, rows), F32)],
        flops=6 * classes * rows * depth,
        moved=4 * rows * depth,
        name="apply_half",
    )


def total_of(values):
    def kernel(*refs):
        value = refs[0][...]
        for ref in refs[1:-1]:
            value = value + ref[...]
        refs[-1][...] = value

    return call(kernel, of(values[0].shape), list(values), mib=4, name="total_of")


def add(lefts, rights, joined=False):
    classes, lanes = lefts[0].shape
    count = len(lefts)
    cover = len(rights) != count

    def kernel(*refs):
        given, outs = refs[: count + len(rights)], refs[count + len(rights) :]
        for k in range(count):
            span = slice(k * lanes, (k + 1) * lanes)
            value = given[k][...] + (given[count][:, span] if cover else given[count + k][...])
            if joined:
                outs[0][:, span] = value
            else:
                outs[k][...] = value

    out = [of((classes, count * lanes))] if joined else [of((classes, lanes))] * count
    return call(kernel, out, list(lefts) + list(rights), mib=4, moved=12 * classes * lanes * count, name="add")


def updated(weights, deltas, table, span):
    kinds, rows = weights.shape
    classes = deltas[0].shape[0]
    seen = seen_lanes(span)
    count = len(deltas)

    def kernel(table_ref, weights_ref, *refs):
        given, (out_ref, window_ref, current, sem) = refs[:count], refs[count:]
        copy = pltpu.make_async_copy(weights_ref, current, sem)
        copy.start()
        copy.wait()
        for k in range(count):
            start, shift = window_at(table_ref[k], seen // LANES, rows)
            value = jnp.concatenate([given[k][...], jnp.zeros((classes, seen - span), F32)], axis=1)
            at = pl.ds(start, seen)
            current[:, at] = current[:, at] + pltpu.roll(value, shift, 1)[:kinds]
        copy = pltpu.make_async_copy(current, out_ref, sem)
        copy.start()
        start, unused = window_at(table_ref[count], seen // LANES, rows)
        window_ref[...] = current[:, pl.ds(start, seen)]
        copy.wait()

    return pl.pallas_call(
        kernel,
        in_specs=[SMEM, HBM] + [VMEM] * count,
        out_specs=[HBM, VMEM],
        out_shape=[of((kinds, rows)), of((kinds, seen))],
        scratch_shapes=[pltpu.VMEM((kinds, rows), F32), pltpu.SemaphoreType.DMA],
        compiler_params=params(8),
        name="updated",
    )(table, weights, *deltas)


def finish(current, before, sides, table, ids, index):
    kinds, rows = current.shape
    classes = sides.flat[0].shape[0]
    span = sides.span
    seen = seen_lanes(span)
    flat = sides.flat

    def kernel(table_ref, ids_ref, current_ref, before_ref, *refs):
        given, (out_ref, value_ref, buffer, sem) = refs[: len(flat)], refs[len(flat) :]
        sides.fill(given, value_ref, ids_ref)
        start, shift = window_at(table_ref[index], seen // LANES, rows)
        value = jnp.concatenate([value_ref[...], jnp.zeros((classes, seen - span), F32)], axis=1)
        buffer[...] = before_ref[...] + pltpu.roll(value, shift, 1)[:kinds]
        copy = pltpu.make_async_copy(buffer, out_ref.at[:, pl.ds(start, seen)], sem)
        copy.start()
        copy.wait()

    return pl.pallas_call(
        kernel,
        in_specs=[SMEM, SMEM, HBM] + [VMEM] * (1 + len(flat)),
        out_specs=HBM,
        out_shape=of((kinds, rows)),
        input_output_aliases={2: 0},
        scratch_shapes=[
            pltpu.VMEM((classes, span), F32),
            pltpu.VMEM((kinds, seen), F32),
            pltpu.SemaphoreType.DMA,
        ],
        compiler_params=params(6),
        name="finish",
    )(table, ids, current, before, *flat)


def rotations(masks, count):
    return [masks[k % len(masks) :] + masks[: k % len(masks)] for k in range(count)]


class Windows:
    def __init__(self):
        self.have, self.queue = {}, []

    def later(self, key, cost, anchor, needs, run, loose=False):
        self.queue.append((key, cost, anchor, needs, run, loose))

    def chosen(self, budget, forced):
        picked, known = [], set(self.have)
        for entry in list(self.queue):
            key, cost, anchor, needs, run, loose = entry
            if not set(needs) <= known:
                continue
            if key in forced or cost <= budget:
                budget -= cost
                picked.append(entry)
                known.add(key)
                self.queue.remove(entry)
        return picked

    def around(self, values, transfer, budget, forced=()):
        picked = self.chosen(budget, forced)
        anchors = [entry[2] for entry in picked if entry[2] in self.have]
        anchors = list(dict.fromkeys(anchors))
        values, tied = lax.optimization_barrier((values, [self.have[key] for key in anchors]))
        self.have.update(zip(anchors, tied))
        got = transfer(values)
        for key, cost, anchor, needs, run, loose in picked:
            self.have[key] = run()
        held = [entry[0] for entry in picked if not entry[5]]
        (values, got), kept = lax.optimization_barrier(((values, got), [self.have[key] for key in held]))
        self.have.update(zip(held, kept))
        return values, got


def body(features, labels, weights, block_order, block_starts, inverses):
    rows, width = features.shape
    updates, span, stretch_rows = inverses.shape
    kinds = weights.shape[1]
    shards, groups = lax.axis_size("samples"), lax.axis_size("cols")
    piece = stretch_rows // shards
    window = max(piece, LANES)
    classes = up(kinds, 8)
    scale = 1.0 / math.sqrt(rows * shards)
    factor = 2.0 / (width * math.log(2.0))
    ids = jnp.stack([lax.axis_index("samples"), lax.axis_index("cols")]).astype(I32)
    turned, weights, labels = features.T, weights.T, labels.reshape(rows // LANES, LANES)

    def place(ids_ref, mask):
        shard = ids_ref[0]
        return shard ^ mask ^ (shard % 2 * (shards // 2))

    def slot(*refs):
        return place(refs[-1], 0) * piece // window

    def inside(*refs):
        return place(refs[-1], 0) * piece % window

    far = list(range(2, shards, 2))
    masks = [0] + far + [1 ^ mask for mask in [0] + far]
    sample_masks = [1 << bit for bit in range(1, shards.bit_length() - 1)]
    col_masks = [1 << bit for bit in range(groups.bit_length() - 1)]
    sample_orders, col_orders = rotations(sample_masks, 2), rotations(col_masks, 2)
    placed = span // groups % LANES == 0
    lanes = span // groups if placed else span // 2
    later_steps = list(range(1, updates))
    batches = [later_steps[:1], later_steps[1:]]
    batch_of = {step: k for k, batch in enumerate(batches) for step in batch}

    def spread(mine):
        return [mine] + [swap(mine, "samples", mask) for mask in far]

    def joined(mine, other, sets):
        pieces = mine + other
        if piece % LANES == 0:
            return assemble(pieces, ids, lambda ids_ref, index: place(ids_ref, masks[index]), sets, piece)
        order = jnp.zeros((shards,), I32).at[place(ids, jnp.array(masks))].set(jnp.arange(shards))
        stacked = jnp.stack(pieces)[order]
        depth = stacked.shape[1]
        return [
            stacked[:, :, k * piece : (k + 1) * piece].transpose(1, 0, 2).reshape(depth, stretch_rows)
            for k in range(sets)
        ]

    def partner(values):
        return [swap(value, "samples", 1) for value in values]

    flow = Windows()
    have = flow.have
    table, query = begin(block_order, block_starts, ids, turned, updates, piece)
    have["table"], have["ids"] = table, ids

    def queue_own(step):
        flow.later(
            ("base", step),
            0.8,
            "table",
            ["table"],
            lambda: own_terms(
                weights, labels, have["table"], ids, updates + step, classes, piece, window, stretch_rows, place
            ),
        )

    def queue_split(step):
        flow.later(("inverse", step), 1.0, "ids", [], lambda: split_inverse(inverses, step, have["ids"]))

    def queue_heavy(step, cuts):
        count = len(cuts) - 1
        for k in range(count):

            def run(k=k):
                have["base", step] = heavy(
                    *have["keys"], have["stretch", step], have["base", step], factor, scale, cuts[k], cuts[k + 1]
                )
                return have["base", step][0]

            needs = [("stretch", step), ("base", step), "keys"] + ([("heavy", step, k - 1)] if k else [])
            key = ("heavy", step) if k == count - 1 else ("heavy", step, k)
            flow.later(key, 7.5 / count, ("base", step), needs, run)

    def queue_tile(step, later):
        flow.later(
            ("tile", step, later),
            0.8,
            "members",
            ["members", ("stretch", later)],
            lambda: tile_of(have["members"], step, have["stretch", later], factor),
        )

    def correction(step, later, sides):
        def offset(table_ref, ids_ref):
            return table_ref[updates + later] - table_ref[step]

        *base, delta = correct(
            have["base", later],
            sides,
            have["tile", step, later],
            [have["table"], ids],
            offset,
            slot,
            inside,
            piece,
            window,
            scale,
        )
        have["base", later] = base
        return delta

    def queue_correction(step, later):
        def run():
            correction(step, later, Sides([[have["delta", step]]], False))
            return have["base", later][0]

        needs = [("delta", step), ("tile", step, later), ("heavy", later)]
        flow.later(("correct", step, later), 1.4, ("delta", step), needs, run)

    def queue_far(batch):
        flow.later(("far", batch), 2.0, ("query", batch), [("query", batch)], lambda: spread(have["query", batch]), True)

    def queue_join(batch):
        steps = batches[batch]

        def run():
            pieces = have["far", batch]
            for step, value in zip(steps, joined(pieces, partner(pieces), len(steps))):
                have["stretch", step] = value
            return have["stretch", steps[0]]

        flow.later(("stretch", steps[0]), 2.5, ("far", batch), [("far", batch)], run)
        for step in steps[1:]:
            flow.later(("stretch", step), 0.0, None, [("stretch", steps[0])], lambda step=step: have["stretch", step])

    def run_queries():
        sets = [[updates + step for step in batch] for batch in batches if batch]
        for k, value in enumerate(query_rows(turned, have["table"], sets, piece)):
            have["query", k] = value
        return have["query", 0]

    flow.later("keys", 3.5, "table", [], lambda: prepare(turned, weights, classes))
    queue_own(0)
    if later_steps:
        flow.later("queries", 2.0, "table", ["table"], run_queries)
    query, pieces = flow.around(query, spread, 100.0)
    queue_split(0)
    pieces, others = flow.around(pieces, partner, 1.0)
    (have["stretch", 0],) = joined(pieces, others, 1)
    if later_steps:
        tied = lax.optimization_barrier((have["stretch", 0], have["query", 0]))
        have["stretch", 0], have["query", 0] = tied
        have["far", 0] = spread(have["query", 0])
        queue_join(0)
    have["base", 0] = heavy(*have["keys"], have["stretch", 0], have["base", 0], factor, scale, 0, rows)

    for step in later_steps:
        queue_own(step)
        if step == 1:
            flow.later("members", 2.6, "table", ["table"], lambda: key_rows(turned, have["table"], updates - 1, span))
        queue_heavy(step, [0, rows // 2, rows])
        if step == 2:
            queue_join(1)
        for before in range(step):
            queue_tile(before, step)
            if before < step - 1:
                queue_correction(before, step)
        queue_split(step)

    for step in range(updates):
        a, b, send = have["base", step]
        follow = step + 1
        forced = [("stretch", follow), ("base", follow)]
        (a, b, send), got = flow.around((a, b, send), lambda values: swap(values[2], "samples", 1), 1.0, forced)
        parts = add([a, b], [got])
        for turn in range(len(sample_orders[0])):
            if turn:
                parts = add(parts, got)
            parts, got = flow.around(
                parts,
                lambda values: [swap(value, "samples", order[turn]) for value, order in zip(values, sample_orders)],
                4.6,
            )
        (residual,) = add(parts, got, joined=True)
        mine_high, mine_low, other_high, other_low = have["inverse", step]
        other = swap(residual, "samples", 1)
        partial = apply_half(mine_high, mine_low, [[residual]], None, span, ids, False)
        parts = apply_half(other_high, other_low, [[other]], partial, lanes, ids, placed)
        forced = []
        if step == 0 and batches[1]:
            queue_far(1)
            forced = [("far", 1)]
        due = [entry[0] for entry in flow.queue if entry[0] in [("heavy", follow, k) for k in range(2)]]
        due += [("heavy", follow), ("inverse", follow), "members", ("tile", step, follow)]
        due += [(kind, before, follow) for kind in ("tile", "correct") for before in range(step)]
        if placed:
            others = list(range(1, groups))
            parts, got = flow.around(
                parts, lambda values: [swap(values[mask], "cols", mask) for mask in others], 5.5, forced
            )
            own = total_of([parts[0]] + list(got))
            own, got = flow.around(own, lambda value: [swap(value, "cols", mask) for mask in others], 5.5, due)
            sides = Sides([[own]] + [[value] for value in got], True)
        else:
            rounds = len(col_orders[0])
            for turn in range(rounds):
                if turn:
                    parts = add(parts, got)
                parts, got = flow.around(
                    parts,
                    lambda values: [swap(value, "cols", order[turn]) for value, order in zip(values, col_orders)],
                    6.0,
                    forced + (due if turn == rounds - 1 else []),
                )
                forced = []
            sides = Sides([[part, other] for part, other in zip(parts, got)], False)
        if follow < updates:
            have["delta", step] = correction(step, follow, sides)
        if follow == updates - 1:

            def run_updated():
                deltas = [have["delta", before] for before in range(updates - 1)]
                have["current"], have["before"] = updated(weights, deltas, have["table"], span)
                return have["before"]

            flow.later("updated", 4.0, ("delta", step), [("delta", step)], run_updated)
        if follow == updates:
            current = finish(have["current"], have["before"], sides, have["table"], ids, step)
    return current.T


def solution(mesh):
    return jax.shard_map(
        body,
        mesh=mesh,
        in_specs=(
            P("samples", None),
            P("samples"),
            P("samples", None),
            P(),
            P(),
            P(None, "samples", "cols"),
        ),
        out_specs=P("samples", None),
        check_vma=False,
    )
```

```python
import math

import jax
import jax.numpy as jnp
from jax import lax
from jax.experimental import pallas as pl
from jax.experimental.pallas import tpu as pltpu
from jax.sharding import PartitionSpec as P

RIDGE = 0.5
F32, BF16, I32 = jnp.float32, jnp.bfloat16, jnp.int32
LANES = 128
VMEM = pl.BlockSpec(memory_space=pltpu.VMEM)
SMEM = pl.BlockSpec(memory_space=pltpu.SMEM)
NT = (((1,), (1,)), ((), ()))


def up(value, unit):
    return -(-value // unit) * unit


def of(shape, kind=F32):
    return jax.ShapeDtypeStruct(shape, kind)


def swap(value, axis, mask):
    size = lax.axis_size(axis)
    return lax.ppermute(value, axis, [(i, i ^ mask) for i in range(size)])


def params(mib, **more):
    return pltpu.CompilerParams(vmem_limit_bytes=mib << 20, **more)


def call(kernel, out, operands, specs=None, mib=8, scratch=(), flops=0, exps=0, moved=0, aliases=None, name=None):
    count = len(operands)
    return pl.pallas_call(
        kernel,
        out_shape=out,
        in_specs=specs or [VMEM] * count,
        out_specs=jax.tree.map(lambda _: VMEM, out),
        scratch_shapes=list(scratch),
        input_output_aliases=aliases or {},
        compiler_params=params(mib),
        cost_estimate=pl.CostEstimate(flops=flops, transcendentals=exps, bytes_accessed=moved),
        name=name,
    )(*operands)


def halves_of_norm(wide):
    value = -0.5 * jnp.sum(wide * wide, axis=0, keepdims=True)
    high = value.astype(BF16).astype(F32)
    middle = (value - high).astype(BF16).astype(F32)
    return high, middle, value - high - middle


def extended(wide, query):
    row = lax.broadcasted_iota(I32, (8, wide.shape[1]), 0)
    tail = jnp.zeros(row.shape, F32)
    first = 3 if query else 0
    for k, part in enumerate(halves_of_norm(wide)):
        tail = jnp.where(row == first + k, part, tail)
        tail = jnp.where(row == 3 - first + k, 1.0, tail)
    return jnp.concatenate([wide, tail], axis=0)


HBM = pl.BlockSpec(memory_space=pltpu.HBM)


def window_at(first, count, total):
    block = jnp.minimum(first // LANES, total // LANES - count)
    return pl.multiple_of(block * LANES, LANES), first - block * LANES


def fetch(source, buffer, sem, start):
    copy = pltpu.make_async_copy(source.at[:, pl.ds(start, buffer.shape[1])], buffer, sem)
    copy.start()
    copy.wait()


def select_query(buffer, shift, count):
    wide = extended(buffer[...].astype(F32), True).astype(BF16)
    shape = (buffer.shape[1], count)
    lane = lax.broadcasted_iota(I32, shape, 0)
    member = lax.broadcasted_iota(I32, shape, 1)
    chosen = jnp.where(lane == member + shift, 1.0, 0.0).astype(BF16)
    return jnp.dot(wide, chosen, preferred_element_type=F32).astype(BF16)


def seen_lanes(count):
    return (up(count, LANES) // LANES + 1) * LANES


def queries(order, starts, turned, updates, piece):
    width, rows = turned.shape
    seen = seen_lanes(piece)

    def kernel(order_hbm, starts_hbm, turned_ref, first_ref, *refs):
        rest, (order_ref, starts_ref, buffers, sems) = refs[:-4], refs[-4:]
        copies = [
            pltpu.make_async_copy(order_hbm, order_ref, sems.at[updates]),
            pltpu.make_async_copy(starts_hbm, starts_ref, sems.at[updates + 1]),
        ]
        for copy in copies:
            copy.start()
        for copy in copies:
            copy.wait()
        copies, shifts = [], []
        for step in range(updates):
            first = starts_ref[order_ref[step]] + lax.axis_index("cols") * piece
            start, shift = window_at(first, seen // LANES, rows)
            source = turned_ref.at[:, pl.ds(start, seen)]
            copies.append(pltpu.make_async_copy(source, buffers.at[step], sems.at[step]))
            shifts.append(shift)
        for copy in copies:
            copy.start()
        for step in range(updates):
            copies[step].wait()
            value = select_query(buffers.at[step], shifts[step], piece)
            if step == 0:
                first_ref[...] = value
            else:
                rest[0][:, (step - 1) * piece : step * piece] = value

    shapes = [(width + 8, piece)] + [(width + 8, (updates - 1) * piece)] * (updates > 1)
    return pl.pallas_call(
        kernel,
        in_specs=[HBM] * 3,
        out_specs=[VMEM] * len(shapes),
        out_shape=[of(shape, BF16) for shape in shapes],
        scratch_shapes=[
            pltpu.SMEM(order.shape, I32),
            pltpu.SMEM(starts.shape, I32),
            pltpu.VMEM((updates, width, seen), BF16),
            pltpu.SemaphoreType.DMA((updates + 2,)),
        ],
        compiler_params=params(60),
        name="queries",
    )(order, starts, turned)


def starts_table(order, starts, updates, piece):
    def kernel(order_ref, starts_ref, out_ref):
        for step in range(updates):
            first = starts_ref[order_ref[step]]
            out_ref[step] = first
            out_ref[updates + step] = first + lax.axis_index("cols") * piece

    return pl.pallas_call(
        kernel,
        in_specs=[SMEM] * 2,
        out_specs=SMEM,
        out_shape=of((2 * updates,), I32),
        compiler_params=params(1),
        name="starts_table",
    )(order, starts)


def key_rows(turned, table, count, span):
    width, rows = turned.shape
    seen = seen_lanes(span)

    def kernel(table_ref, turned_ref, out_ref, buffer, sem):
        def step(index, carry):
            start, shift = window_at(table_ref[index], seen // LANES, rows)
            fetch(turned_ref, buffer, sem, start)
            wide = extended(buffer[...].astype(F32), False).astype(BF16)
            member = lax.broadcasted_iota(I32, (span, seen), 0)
            lane = lax.broadcasted_iota(I32, (span, seen), 1)
            chosen = jnp.where(lane == member + shift, 1.0, 0.0).astype(BF16)
            rows_of = lax.dot_general(chosen, wide, NT, preferred_element_type=F32)
            out_ref[pl.ds(index, 1)] = rows_of.astype(BF16)[None]
            return carry

        lax.fori_loop(0, count, step, 0)

    return call(
        kernel,
        of((count, span, width + 8), BF16),
        [table, turned],
        [SMEM, HBM],
        mib=8,
        scratch=[pltpu.VMEM((width, seen), BF16), pltpu.SemaphoreType.DMA],
        name="key_rows",
    )


def own_terms(weights, labels, table, index, classes, piece, window, columns, place):
    kinds, rows = weights.shape
    seen = 2 * LANES
    half, quarter = columns // 2, columns // 4
    last = labels.shape[0] - 1

    def kernel(table_ref, labels_ref, weights_ref, a_ref, b_ref, send_ref, placed, buffer, sem):
        first = table_ref[index]
        start, shift = window_at(first, 2, rows)
        fetch(weights_ref, buffer, sem, start)
        lane_at = place(0) * piece
        inside = lane_at % window
        turn = (inside - shift + 2 * seen) % seen
        both = pltpu.roll(buffer[...], turn, 1)[:, :LANES]
        block = start // LANES
        lines = [labels_ref[pl.ds(block + k, 1), :] for k in range(2)]
        lines = jnp.broadcast_to(jnp.concatenate(lines, axis=1), (8, seen))
        label = pltpu.roll(lines, turn, 1)[:1, :LANES]
        hot = jnp.where(lax.broadcasted_iota(I32, (kinds, LANES), 0) == label, 1.0, 0.0)
        lane = lax.broadcasted_iota(I32, (kinds, LANES), 1) - inside
        value = jnp.where((lane >= 0) & (lane < piece), hot - RIDGE * both, 0.0)
        placed[...] = jnp.zeros_like(placed)
        placed[:kinds, pl.ds(pl.multiple_of(lane_at // window * window, LANES), LANES)] = value
        a_ref[...] = placed[:, :quarter]
        b_ref[...] = placed[:, quarter:half]
        send_ref[...] = placed[:, half:]

    assert window == LANES
    return call(
        kernel,
        [of((classes, quarter)), of((classes, quarter)), of((classes, half))],
        [table, labels, weights],
        [SMEM, VMEM, HBM],
        mib=4,
        scratch=[
            pltpu.VMEM((classes, columns), F32),
            pltpu.VMEM((kinds, seen), F32),
            pltpu.SemaphoreType.DMA,
        ],
        name="own_terms",
    )


def prepare(turned, weights, classes):
    width, rows = turned.shape
    kinds = weights.shape[0]
    depth, block = width + 8, 512

    def kernel(turned_ref, weights_ref, keys_ref, parts_ref):
        wide = extended(turned_ref[...].astype(F32), False)
        keys_ref[...] = wide.T.astype(BF16)
        value = jnp.concatenate([weights_ref[...], jnp.zeros((classes - kinds, block), F32)], axis=0)
        high = value.astype(BF16).astype(F32)
        parts_ref[...] = jnp.concatenate([high, value - high], axis=0).astype(BF16)

    return pl.pallas_call(
        kernel,
        grid=(rows // block,),
        in_specs=[
            pl.BlockSpec((width, block), lambda i: (0, i)),
            pl.BlockSpec((kinds, block), lambda i: (0, i)),
        ],
        out_specs=[
            pl.BlockSpec((block, depth), lambda i: (i, 0)),
            pl.BlockSpec((2 * classes, block), lambda i: (0, i)),
        ],
        out_shape=[of((rows, depth), BF16), of((2 * classes, rows), BF16)],
        compiler_params=params(12, dimension_semantics=("arbitrary",)),
        cost_estimate=pl.CostEstimate(flops=1 << 20, transcendentals=0, bytes_accessed=8 << 20),
        name="prepare",
    )(turned, weights)


def split_inverse(inverses, index):
    rows, columns = inverses.shape[1:]
    half = columns // 2
    block = min(rows, 128)
    count = rows // block

    def kernel(inverse_ref, *refs):
        outs, (buffer, sems) = refs[:4], refs[4:]
        core = lax.axis_index("samples") % 2
        copies = [
            pltpu.make_async_copy(
                inverse_ref.at[index, pl.ds(k * block, block)], buffer.at[pl.ds(k * block, block)], sems.at[k]
            )
            for k in range(count)
        ]
        for copy in copies:
            copy.start()
        for i in range(count):
            copies[i].wait()
            at = slice(i * block, (i + 1) * block)
            for k in range(2):
                side = pl.multiple_of((core + k) % 2 * half, LANES)
                value = buffer[at, pl.ds(side, half)]
                high = value.astype(BF16)
                outs[2 * k][at, :] = high
                outs[2 * k + 1][at, :] = (value - high.astype(F32)).astype(BF16)

    return pl.pallas_call(
        kernel,
        in_specs=[HBM],
        out_specs=[VMEM] * 4,
        out_shape=[of((rows, half), BF16)] * 4,
        scratch_shapes=[pltpu.VMEM((rows, columns), F32), pltpu.SemaphoreType.DMA((count,))],
        compiler_params=params(10),
        cost_estimate=pl.CostEstimate(flops=1 << 20, transcendentals=0, bytes_accessed=8 * rows * columns),
        name="split_inverse",
    )(inverses)


def assemble(pieces, place, sets, lanes):
    count = len(pieces)
    depth = pieces[0].shape[0]

    def kernel(*refs):
        for index in range(count):
            start = pl.multiple_of(place(index) * lanes, LANES)
            for k in range(sets):
                refs[count + k][:, pl.ds(start, lanes)] = refs[index][:, k * lanes : (k + 1) * lanes]

    out = [of((depth, count * lanes), BF16)] * sets
    return call(kernel, out, pieces, mib=10, name="assemble")


def heavy(keys, parts, stretch, base, factor, scale, first, last):
    rows, depth = last - first, keys.shape[1]
    columns = stretch.shape[1]
    half = columns // 2
    quarter = half // 2
    doubled = parts.shape[0]
    classes = doubled // 2
    block = min(rows, 1024)
    side = block // 2
    wide = min(256, columns)

    def kernel(keys_ref, parts_ref, stretch_ref, a_in, b_in, send_in, a_ref, b_ref, send_ref, total, front, back):
        def fill(panel, start):
            lhs = keys_ref[pl.ds(first + start, side), :]
            for j in range(columns // wide):
                span = slice(j * wide, (j + 1) * wide)
                inner = jnp.dot(lhs, stretch_ref[:, span], preferred_element_type=F32)
                panel[:, span] = jnp.exp2(inner * factor).astype(BF16)

        def drain(panel, start):
            lhs = parts_ref[:, pl.ds(first + start, side)]
            for j in range(columns // wide):
                span = slice(j * wide, (j + 1) * wide)
                total[:, span] += jnp.dot(lhs, panel[:, span], preferred_element_type=F32)

        total[...] = jnp.zeros_like(total)
        fill(front, 0)

        def step(i, carry):
            start = pl.multiple_of(i * block, block)
            fill(back, start + side)
            drain(front, start)
            fill(front, start + block)
            drain(back, start + side)
            return carry

        lax.fori_loop(0, rows // block - 1, step, 0)
        fill(back, rows - side)
        drain(front, rows - block)
        drain(back, rows - side)
        spans = [slice(0, quarter), slice(quarter, half), slice(half, columns)]
        for span, given, out in zip(spans, (a_in, b_in, send_in), (a_ref, b_ref, send_ref)):
            out[...] = given[...] - scale * (total[:classes, span] + total[classes:, span])

    return call(
        kernel,
        [of((classes, quarter)), of((classes, quarter)), of((classes, half))],
        [keys, parts, stretch] + list(base),
        mib=16,
        scratch=[
            pltpu.VMEM((doubled, columns), F32),
            pltpu.VMEM((side, columns), BF16),
            pltpu.VMEM((side, columns), BF16),
        ],
        flops=2 * rows * columns * (depth + doubled),
        exps=rows * columns,
        moved=2 * rows * (depth + doubled) + 2 * columns * depth,
        name="heavy",
    )


def tile_of(members, index, stretch, table, later, updates, factor, piece, window, place):
    rows, depth = members.shape[1:]
    columns = stretch.shape[1]
    wide = min(512, columns)

    def kernel(table_ref, members_ref, stretch_ref, out_ref, pick_ref):
        def step(j, carry):
            span = pl.ds(pl.multiple_of(j * wide, wide), wide)
            inner = jnp.dot(members_ref[index], stretch_ref[:, span], preferred_element_type=F32)
            out_ref[:, span] = jnp.exp2(inner * factor).astype(BF16)
            return carry

        lax.fori_loop(0, columns // wide, step, 0)
        offset = table_ref[updates + later] - table_ref[index]
        row = lax.broadcasted_iota(I32, (rows, window), 0)
        lane = lax.broadcasted_iota(I32, (rows, window), 1) - place(0) * piece % window
        match = (row == lane + offset) & (lane >= 0) & (lane < piece)
        pick_ref[...] = jnp.where(match, 1.0, 0.0).astype(BF16)

    return call(
        kernel,
        [of((rows, columns), BF16), of((rows, window), BF16)],
        [table, members, stretch],
        [SMEM, VMEM, VMEM],
        flops=2 * rows * columns * depth,
        exps=rows * columns,
        moved=2 * rows * (columns + depth) + 2 * columns * depth,
        name="tile",
    )


class Sides:
    def __init__(self, parts, placed):
        self.parts, self.placed = parts, placed
        self.flat = [value for part in parts for value in part]
        self.lanes = parts[0][0].shape[1]
        self.span = self.lanes * len(parts)

    def fill(self, given, out):
        at = 0
        for k, part in enumerate(self.parts):
            value = given[at][...]
            for more in range(1, len(part)):
                value = value + given[at + more][...]
            at += len(part)
            if self.placed:
                group = lax.axis_index("cols")
                out[:, pl.ds(pl.multiple_of((group ^ k) * self.lanes, LANES), self.lanes)] = value
            else:
                out[:, k * self.lanes : (k + 1) * self.lanes] = value


def correct(base, sides, tile, pick, place, piece, scale):
    a, b, send = base
    classes, quarter = a.shape
    half = 2 * quarter
    rows, columns = tile.shape
    window = pick.shape[1]
    flat = sides.flat

    def kernel(tile_ref, pick_ref, a_in, b_in, send_in, *refs):
        given = refs[: len(flat)]
        a_ref, b_ref, send_ref, delta_ref, sums = refs[len(flat) :]
        sides.fill(given, delta_ref)
        delta = delta_ref[...]
        high = delta.astype(BF16)
        rest = delta - high.astype(F32)
        middle = rest.astype(BF16)
        low = (rest - middle.astype(F32)).astype(BF16)
        both = jnp.concatenate([high, middle], axis=0)
        product = jnp.dot(both, tile_ref[...], preferred_element_type=F32)
        sums[...] = -scale * (product[:classes] + product[classes:])
        picked = jnp.dot(jnp.concatenate([both, low], axis=0), pick_ref[...], preferred_element_type=F32)
        picked = picked[:classes] + picked[classes : 2 * classes] + picked[2 * classes :]
        span = pl.ds(pl.multiple_of(place(0) * piece // window * window, LANES), window)
        sums[:, span] = sums[:, span] - RIDGE * picked
        a_ref[...] = a_in[...] + sums[:, :quarter]
        b_ref[...] = b_in[...] + sums[:, quarter:half]
        send_ref[...] = send_in[...] + sums[:, half:]

    return call(
        kernel,
        [of(a.shape), of(b.shape), of(send.shape), of((classes, rows))],
        [tile, pick, a, b, send] + flat,
        mib=10,
        scratch=[pltpu.VMEM((classes, columns), F32)],
        flops=4 * classes * rows * columns,
        moved=2 * rows * columns,
        name="correct",
    )


def apply_half(high, low, sides, start, lanes, placed):
    classes = sides[0][0].shape[0]
    rows, depth = high.shape
    count = rows // lanes
    flat = [value for part in sides for value in part]
    begun = list(start or [])

    def kernel(high_ref, low_ref, *refs):
        given, before = refs[: len(flat)], refs[len(flat) : len(flat) + len(begun)]
        outs, whole = refs[len(flat) + len(begun) : -1], refs[-1]
        at, values = 0, []
        for part in sides:
            value = given[at][...]
            for more in range(1, len(part)):
                value = value + given[at + more][...]
            at += len(part)
            values.append(value)
        value = jnp.concatenate(values, axis=1) if len(values) > 1 else values[0]
        top = value.astype(BF16)
        rest = (value - top.astype(F32)).astype(BF16)
        both = jnp.concatenate([top, rest], axis=0)
        product = lax.dot_general(both, high_ref[...], NT, preferred_element_type=F32)
        total = product[:classes] + product[classes:]
        total = total + lax.dot_general(top, low_ref[...], NT, preferred_element_type=F32)
        if begun:
            total = total + before[0][...]
        if placed:
            whole[...] = total
        for k in range(count):
            if placed:
                at = pl.ds(pl.multiple_of((lax.axis_index("cols") ^ k) * lanes, LANES), lanes)
                outs[k][...] = whole[:, at]
            else:
                outs[k][...] = total[:, k * lanes : (k + 1) * lanes]

    return call(
        kernel,
        [of((classes, lanes))] * count,
        [high, low] + flat + begun,
        mib=8,
        scratch=[pltpu.VMEM((classes, rows), F32)],
        flops=6 * classes * rows * depth,
        moved=4 * rows * depth,
        name="apply_half",
    )


def total_of(values):
    def kernel(*refs):
        value = refs[0][...]
        for ref in refs[1:-1]:
            value = value + ref[...]
        refs[-1][...] = value

    return call(kernel, of(values[0].shape), list(values), mib=4, name="total_of")


def add(lefts, rights, joined=False):
    classes, lanes = lefts[0].shape
    count = len(lefts)
    cover = len(rights) != count

    def kernel(*refs):
        given, outs = refs[: count + len(rights)], refs[count + len(rights) :]
        for k in range(count):
            span = slice(k * lanes, (k + 1) * lanes)
            value = given[k][...] + (given[count][:, span] if cover else given[count + k][...])
            if joined:
                outs[0][:, span] = value
            else:
                outs[k][...] = value

    out = [of((classes, count * lanes))] if joined else [of((classes, lanes))] * count
    return call(kernel, out, list(lefts) + list(rights), mib=4, moved=12 * classes * lanes * count, name="add")


def updated(weights, deltas, table, span):
    kinds, rows = weights.shape
    classes = deltas[0].shape[0]
    seen = seen_lanes(span)
    count = len(deltas)

    def kernel(table_ref, weights_ref, *refs):
        given, (out_ref, window_ref, current, sem) = refs[:count], refs[count:]
        copy = pltpu.make_async_copy(weights_ref, current, sem)
        copy.start()
        copy.wait()
        for k in range(count):
            start, shift = window_at(table_ref[k], seen // LANES, rows)
            value = jnp.concatenate([given[k][...], jnp.zeros((classes, seen - span), F32)], axis=1)
            at = pl.ds(start, seen)
            current[:, at] = current[:, at] + pltpu.roll(value, shift, 1)[:kinds]
        copy = pltpu.make_async_copy(current, out_ref, sem)
        copy.start()
        start, unused = window_at(table_ref[count], seen // LANES, rows)
        window_ref[...] = current[:, pl.ds(start, seen)]
        copy.wait()

    return pl.pallas_call(
        kernel,
        in_specs=[SMEM, HBM] + [VMEM] * count,
        out_specs=[HBM, VMEM],
        out_shape=[of((kinds, rows)), of((kinds, seen))],
        scratch_shapes=[pltpu.VMEM((kinds, rows), F32), pltpu.SemaphoreType.DMA],
        compiler_params=params(8),
        name="updated",
    )(table, weights, *deltas)


def finish(current, before, sides, table, index):
    kinds, rows = current.shape
    classes = sides.flat[0].shape[0]
    span = sides.span
    seen = seen_lanes(span)
    flat = sides.flat

    def kernel(table_ref, current_ref, before_ref, *refs):
        given, (out_ref, value_ref, buffer, sem) = refs[: len(flat)], refs[len(flat) :]
        sides.fill(given, value_ref)
        start, shift = window_at(table_ref[index], seen // LANES, rows)
        value = jnp.concatenate([value_ref[...], jnp.zeros((classes, seen - span), F32)], axis=1)
        buffer[...] = before_ref[...] + pltpu.roll(value, shift, 1)[:kinds]
        copy = pltpu.make_async_copy(buffer, out_ref.at[:, pl.ds(start, seen)], sem)
        copy.start()
        copy.wait()

    return pl.pallas_call(
        kernel,
        in_specs=[SMEM, HBM] + [VMEM] * (1 + len(flat)),
        out_specs=HBM,
        out_shape=of((kinds, rows)),
        input_output_aliases={1: 0},
        scratch_shapes=[
            pltpu.VMEM((classes, span), F32),
            pltpu.VMEM((kinds, seen), F32),
            pltpu.SemaphoreType.DMA,
        ],
        compiler_params=params(6),
        name="finish",
    )(table, current, before, *flat)


def rotations(masks, count):
    return [masks[k % len(masks) :] + masks[: k % len(masks)] for k in range(count)]


class Windows:
    def __init__(self):
        self.have, self.queue = {}, []

    def later(self, key, cost, anchor, needs, run, loose=False):
        self.queue.append((key, cost, anchor, needs, run, loose))

    def chosen(self, budget, forced):
        picked, known = [], set(self.have)
        for entry in list(self.queue):
            key, cost, anchor, needs, run, loose = entry
            if not set(needs) <= known:
                continue
            if key in forced or cost <= budget:
                budget -= cost
                picked.append(entry)
                known.add(key)
                self.queue.remove(entry)
        return picked

    def around(self, values, transfer, budget, forced=()):
        picked = self.chosen(budget, forced)
        anchors = [entry[2] for entry in picked if entry[2] is not None and entry[2] in self.have]
        anchors = list(dict.fromkeys(anchors))
        values, tied = lax.optimization_barrier((values, [self.have[key] for key in anchors]))
        self.have.update(zip(anchors, tied))
        got = transfer(values)
        for key, cost, anchor, needs, run, loose in picked:
            self.have[key] = run()
        held = [entry[0] for entry in picked if not entry[5]]
        (values, got), kept = lax.optimization_barrier(((values, got), [self.have[key] for key in held]))
        self.have.update(zip(held, kept))
        return values, got


def body(features, labels, weights, block_order, block_starts, inverses):
    rows, width = features.shape
    updates, span, stretch_rows = inverses.shape
    kinds = weights.shape[1]
    shards, groups = lax.axis_size("samples"), lax.axis_size("cols")
    piece = stretch_rows // shards
    window = max(piece, LANES)
    classes = up(kinds, 8)
    scale = 1.0 / math.sqrt(rows * shards)
    factor = 2.0 / (width * math.log(2.0))
    turned, weights, labels = features.T, weights.T, labels.reshape(rows // LANES, LANES)

    def place(mask):
        shard = lax.axis_index("samples")
        return shard ^ mask ^ (shard % 2 * (shards // 2))

    far = list(range(2, shards, 2))
    masks = [0] + far + [1 ^ mask for mask in [0] + far]
    sample_masks = [1 << bit for bit in range(1, shards.bit_length() - 1)]
    col_masks = [1 << bit for bit in range(groups.bit_length() - 1)]
    sample_orders, col_orders = rotations(sample_masks, 2), rotations(col_masks, 2)
    placed = span // groups % LANES == 0
    lanes = span // groups if placed else span // 2
    later_steps = list(range(1, updates))

    def spread(mine):
        return [mine] + [swap(mine, "samples", mask) for mask in far]

    def joined(mine, other, sets):
        pieces = mine + other
        if piece % LANES == 0:
            return assemble(pieces, lambda index: place(masks[index]), sets, piece)
        order = jnp.zeros((shards,), I32).at[place(jnp.array(masks))].set(jnp.arange(shards))
        stacked = jnp.stack(pieces)[order]
        depth = stacked.shape[1]
        return [
            stacked[:, :, k * piece : (k + 1) * piece].transpose(1, 0, 2).reshape(depth, stretch_rows)
            for k in range(sets)
        ]

    def partner(values):
        return [swap(value, "samples", 1) for value in values]

    flow = Windows()
    have = flow.have
    query, *rest = queries(block_order, block_starts, turned, updates, piece)
    have["query"] = query

    def queue_own(step):
        flow.later(
            ("base", step),
            0.8,
            "table",
            ["table"],
            lambda: own_terms(
                weights, labels, have["table"], updates + step, classes, piece, window, stretch_rows, place
            ),
        )

    def queue_split(step):
        flow.later(("inverse", step), 1.1, None, [], lambda: split_inverse(inverses, step))

    def queue_heavy(step, cuts):
        count = len(cuts) - 1
        for k in range(count):

            def run(k=k):
                have["base", step] = heavy(
                    *have["keys"], have["stretch", step], have["base", step], factor, scale, cuts[k], cuts[k + 1]
                )
                return have["base", step][0]

            needs = [("stretch", step), ("base", step), "keys"] + ([("heavy", step, k - 1)] if k else [])
            key = ("heavy", step) if k == count - 1 else ("heavy", step, k)
            flow.later(key, 7.5 / count, ("base", step), needs, run)

    def queue_tile(step, later):
        def run():
            return tile_of(
                have["members"],
                step,
                have["stretch", later],
                have["table"],
                later,
                updates,
                factor,
                piece,
                window,
                place,
            )

        flow.later(("tile", step, later), 0.95, "members", ["members", ("stretch", later)], run)

    def correction(step, later, sides):
        *base, delta = correct(have["base", later], sides, *have["tile", step, later], place, piece, scale)
        have["base", later] = base
        return delta

    def queue_correction(step, later):
        def run():
            correction(step, later, Sides([[have["delta", step]]], False))
            return have["base", later][0]

        needs = [("delta", step), ("tile", step, later), ("heavy", later)]
        flow.later(("correct", step, later), 1.4, ("delta", step), needs, run)

    flow.later("table", 0.5, None, [], lambda: starts_table(block_order, block_starts, updates, piece))
    flow.later("keys", 3.0, "query", [], lambda: prepare(turned, weights, classes))
    if rest:
        (query, rest) = lax.optimization_barrier((query, rest))
        have["query"] = query

    def first_spread(query):
        pieces = spread(query)
        if rest:
            have["far"] = spread(rest[0])
        return pieces

    query, pieces = flow.around(query, first_spread, 4.0)
    queue_own(0)
    pieces, others = flow.around(pieces, partner, 1.0)
    (have["stretch", 0],) = joined(pieces, others, 1)
    have["base", 0] = heavy(*have["keys"], have["stretch", 0], have["base", 0], factor, scale, 0, rows)

    def run_join():
        for step, value in zip(later_steps, joined(have["far"], have["swapped"], updates - 1)):
            have["stretch", step] = value
        return have["stretch", 1]

    if later_steps:
        flow.later("swapped", 1.1, "far", ["far"], lambda: partner(have["far"]), True)
        flow.later("members", 2.6, "table", ["table"], lambda: key_rows(turned, have["table"], updates - 1, span))
        flow.later(("stretch", 1), 2.4, "swapped", ["swapped"], run_join)
        for step in later_steps[1:]:
            flow.later(("stretch", step), 0.0, None, [("stretch", 1)], lambda step=step: have["stretch", step])
    queue_split(0)
    for step in later_steps:
        queue_own(step)
        if step > 1:
            for before in range(step):
                queue_tile(before, step)
        queue_heavy(step, [0, rows // 2, rows])
        if step == 1:
            queue_tile(0, 1)
        for before in range(step - 1):
            queue_correction(before, step)
        queue_split(step)

    for step in range(updates):
        a, b, send = have["base", step]
        follow = step + 1
        (a, b, send), got = flow.around((a, b, send), lambda values: swap(values[2], "samples", 1), 0.0)
        parts = add([a, b], [got])
        for turn in range(len(sample_orders[0])):
            if turn:
                parts = add(parts, got)
            parts, got = flow.around(
                parts,
                lambda values: [swap(value, "samples", order[turn]) for value, order in zip(values, sample_orders)],
                3.9,
                [("inverse", step)] if turn else [],
            )
        (residual,) = add(parts, got, joined=True)
        mine_high, mine_low, other_high, other_low = have["inverse", step]
        other = swap(residual, "samples", 1)
        partial = apply_half(mine_high, mine_low, [[residual]], None, span, False)
        parts = apply_half(other_high, other_low, [[other]], partial, lanes, placed)
        due = [entry[0] for entry in flow.queue if entry[0] in [("heavy", follow, k) for k in range(2)]]
        due += [("heavy", follow), "members", ("tile", step, follow)]
        due += [(kind, before, follow) for kind in ("tile", "correct") for before in range(step)]
        if placed:
            others = list(range(1, groups))
            parts, got = flow.around(
                parts, lambda values: [swap(values[mask], "cols", mask) for mask in others], 5.2
            )
            own = total_of([parts[0]] + list(got))
            own, got = flow.around(own, lambda value: [swap(value, "cols", mask) for mask in others], 4.7, due)
            sides = Sides([[own]] + [[value] for value in got], True)
        else:
            rounds = len(col_orders[0])
            for turn in range(rounds):
                if turn:
                    parts = add(parts, got)
                parts, got = flow.around(
                    parts,
                    lambda values: [swap(value, "cols", order[turn]) for value, order in zip(values, col_orders)],
                    6.0,
                    due if turn == rounds - 1 else [],
                )
            sides = Sides([[part, other] for part, other in zip(parts, got)], False)
        if follow < updates:
            have["delta", step] = correction(step, follow, sides)
        if follow == updates - 1:

            def run_updated():
                deltas = [have["delta", before] for before in range(updates - 1)]
                have["current"], have["before"] = updated(weights, deltas, have["table"], span)
                return have["before"]

            flow.later("updated", 4.0, ("delta", step), [("delta", step)], run_updated)
        if follow == updates:
            current = finish(have["current"], have["before"], sides, have["table"], step)
    return current.T


def solution(mesh):
    return jax.shard_map(
        body,
        mesh=mesh,
        in_specs=(
            P("samples", None),
            P("samples"),
            P("samples", None),
            P(),
            P(),
            P(None, "samples", "cols"),
        ),
        out_specs=P("samples", None),
        check_vma=False,
    )
```
